256 devices in a mesh: lon: 32 (over x_lo, z, core), lat: 8 (over x_hi, y).
Axes of the slice: x: 4 (x_hi: 2, x_lo: 2; x = x_hi * 2 + x_lo), y: 4, z: 8, core: 2. Of those that a mesh axis runs over, the one named last changes fastest.
Arguments:
- initial_state: float32 [4, 10, 128, 4096], P(None, None, 'lat', 'lon'), may hold values from -6 to 6
- land_mask: int32 [10, 128, 4096], P(None, 'lat', 'lon'), may hold values from 0 to 1, as said below
- surface_flux: float32 [128, 4096], P('lat', 'lon'), may hold values from 0 to 10, as said below
- weight_in: float32 [40, 64], replicated, may hold values from -1 to 1
- bias_in: float32 [64], replicated, may hold values from -3 to 3
- weight_mid: float32 [64, 64], replicated, may hold values from -0.75 to 0.75
- bias_mid: float32 [64], replicated, may hold values from -3 to 3
- weight_out: float32 [64, 40], replicated, may hold values from -0.75 to 0.75
- bias_out: float32 [40], replicated, may hold values from -3 to 3
- cotangent: float32 [4, 10, 128, 4096], P(None, None, 'lat', 'lon'), may hold values from -6 to 6
Outputs:
- final_state: float32 [4, 10, 128, 4096], P(None, None, 'lat', 'lon')
- state_grad: float32 [4, 10, 128, 4096], P(None, None, 'lat', 'lon')
- grad_weight_in: float32 [40, 64], replicated
- grad_bias_in: float32 [64], replicated
- grad_weight_mid: float32 [64, 64], replicated
- grad_bias_mid: float32 [64], replicated
- grad_weight_out: float32 [64, 40], replicated
- grad_bias_out: float32 [40], replicated
The draws below stay inside these ranges and needn't reach their ends.
Inputs may be any that keep to these rules, and one draw needn't show every extreme that they name: `land_mask`: at every cell the ocean levels are a run from level 0 down; at least one cell is ocean at every level. `surface_flux`: strictly positive.
All inputs are finite; a program needn't handle non-finite values.
Results may differ from the reference program's by a relative error of at most 0.00012.
Values sent between devices are 32-bit elements; how exact they have to be, the bound alone decides.
A program may use at most 128 MiB of HBM per device.

```python
import math
import jax
import jax.numpy as jnp
from jax import lax

LEV = 10
HID = 64
STEPS = 2
NLAT = 128
NLON = 4096
FEAT = 40


def draw_land_mask(key, part):
    roll_key = jax.random.fold_in(key, 11)
    depth_key = jax.random.fold_in(key, 12)
    col_index = jnp.arange(NLON, dtype=jnp.int32)
    row_index = jnp.arange(NLAT, dtype=jnp.int32)
    lon_odds = 300 + 700 * col_index // NLON
    lat_odds = 300 + 700 * row_index // NLAT
    odds = lat_odds[:, None] * lon_odds[None, :] // 1000
    rolled = jax.random.randint(roll_key, (NLAT, NLON), 0, 1000, dtype=jnp.int32)
    depths = jax.random.randint(depth_key, (NLAT, NLON), 1, LEV + 1, dtype=jnp.int32)
    depths = jnp.where(rolled < odds, depths, 0)
    anchor = (row_index[:, None] == NLAT // 2) & (col_index[None, :] == NLON // 2)
    depths = jnp.where(anchor, LEV, depths)
    levels = jnp.arange(LEV, dtype=jnp.int32)
    return (levels[:, None, None] < depths[None, :, :]).astype(jnp.int32)


def draw_surface_flux(key, part):
    row_key = jax.random.fold_in(key, 21)
    col_key = jax.random.fold_in(key, 22)
    cell_key = jax.random.fold_in(key, 23)
    col_scale = jnp.exp(2.302585 * jax.random.uniform(col_key, (1, NLON), jnp.float32))
    cells = jax.random.uniform(cell_key, (NLAT, NLON), jnp.float32)
    row_scale = jnp.exp(2.302585 * jax.random.uniform(row_key, (NLAT, 1), jnp.float32))
    return row_scale * col_scale * (0.5 + cells) / 15.0


def block_scale(stream_key, extent, cuts, smallest, top_value):
    loudness = 1.0
    for axis_at, shards_of in cuts:
        draws = jax.random.uniform(jax.random.fold_in(jax.random.fold_in(stream_key, 6), axis_at), (shards_of,), jnp.float32, smallest / len(cuts), top_value / len(cuts))
        loudness = loudness * jnp.repeat(jnp.exp(draws), extent[axis_at] // shards_of).reshape((-1,) + (1,) * (len(extent) - 1 - axis_at))
    return loudness


def centred(stream_key, dims, scale, limit, cuts=(), kind=jnp.bfloat16):
    values = jax.random.normal(stream_key, dims, jnp.float32) * scale
    if len(cuts) > 0:
        values = block_scale(stream_key, dims, cuts, -0.22, 0.18) * values
    return jnp.clip(values, min=-limit, max=limit).astype(kind)


def setup_inputs(seed: int = 0) -> dict:
    arg_keys = jax.random.split(jax.random.key(seed), 11)
    return {
        "initial_state": centred(arg_keys[0], (4, LEV, NLAT, NLON), 1.0, 6.0, ((2, 8), (3, 32)), jnp.float32),
        "land_mask": draw_land_mask(jax.random.fold_in(arg_keys[10], 71), 0),
        "surface_flux": draw_surface_flux(jax.random.fold_in(arg_keys[10], 71), 0),
        "weight_in": centred(arg_keys[3], (FEAT, HID), FEAT ** -0.5, 1.0, (), jnp.float32),
        "bias_in": centred(arg_keys[4], (HID,), 0.5, 3.0, (), jnp.float32),
        "weight_mid": centred(arg_keys[5], (HID, HID), HID ** -0.5, 0.75, (), jnp.float32),
        "bias_mid": centred(arg_keys[6], (HID,), 0.5, 3.0, (), jnp.float32),
        "weight_out": centred(arg_keys[7], (HID, FEAT), HID ** -0.5, 0.75, (), jnp.float32),
        "bias_out": centred(arg_keys[8], (FEAT,), 0.5, 3.0, (), jnp.float32),
        "cotangent": centred(arg_keys[9], (4, LEV, NLAT, NLON), 1.0, 6.0, ((2, 8), (3, 32)), jnp.float32),
    }


LAT_LIMIT = 1.2
TIME_STEP = 0.25
PRESSURE_GAIN = 0.5
THERMAL_EXPANSION = 0.2
HALINE_CONTRACTION = 0.8
CORIOLIS = 1.0
VISCOSITY = 0.15
DIFFUSIVITY = 0.1
FRESHWATER = 2.0
HIGHEST = lax.Precision.HIGHEST

def pressure_of(fields):
    return PRESSURE_GAIN * jnp.cumsum(HALINE_CONTRACTION * fields[1] - THERMAL_EXPANSION * fields[0], axis=0)

def combine(center, east_side, west_side, north_side, south_side, press_east, press_west, press_north, press_south, ocean_cells, inv_cos, coriolis):
    half_metric = 0.5 * inv_cos
    slope_x = (east_side - west_side) * half_metric
    slope_y = (north_side - south_side) * 0.5
    laplace = (east_side + west_side - 2.0 * center) * (inv_cos * inv_cos) + (north_side + south_side - 2.0 * center)
    along_u = center[2]
    along_v = center[3]
    mixing = jnp.array([DIFFUSIVITY, DIFFUSIVITY, VISCOSITY, VISCOSITY], jnp.float32).reshape((4,) + (1,) * (center.ndim - 1))
    change = mixing * laplace - (along_u * slope_x + along_v * slope_y)
    force_x = coriolis * along_v - (press_east - press_west) * half_metric
    force_y = -coriolis * along_u - (press_north - press_south) * 0.5
    return ocean_cells * jnp.stack([change[0], change[1], change[2] + force_x, change[3] + force_y])

def latitude_terms(row_index, row_count):
    latitude = LAT_LIMIT * (2.0 * (jnp.clip(row_index, 0.0, row_count - 1.0) + 0.5) / row_count - 1.0)
    return ((1.0 / jnp.cos(latitude))[:, None], (CORIOLIS * jnp.sin(latitude))[:, None])

def east_of(fields):
    return jnp.roll(fields, -1, axis=-1)

def west_of(fields):
    return jnp.roll(fields, 1, axis=-1)

def north_of(fields):
    return jnp.concatenate([fields[..., 1:, :], jnp.zeros_like(fields[..., :1, :])], axis=-2)

def south_of(fields):
    return jnp.concatenate([jnp.zeros_like(fields[..., :1, :]), fields[..., :-1, :]], axis=-2)

def dynamics(fields, ocean_cells, inv_cos, coriolis):
    pressure = pressure_of(fields)

    def one_level(pieces):
        column, level_press, level_ocean = pieces
        return combine(column, east_of(column), west_of(column), north_of(column), south_of(column), east_of(level_press), west_of(level_press), north_of(level_press), south_of(level_press), level_ocean, inv_cos, coriolis)
    per_level = lax.map(jax.checkpoint(one_level), (jnp.moveaxis(fields, 1, 0), pressure, ocean_cells))
    return jnp.moveaxis(per_level, 0, 1)

def three_sections(fields, ocean_cells, inv_cos, coriolis):
    section_one = fields + TIME_STEP * dynamics(fields, ocean_cells, inv_cos, coriolis)
    section_two = 0.75 * fields + 0.25 * (section_one + TIME_STEP * dynamics(section_one, ocean_cells, inv_cos, coriolis))
    return 1.0 / 3.0 * fields + 2.0 / 3.0 * (section_two + TIME_STEP * dynamics(section_two, ocean_cells, inv_cos, coriolis))

def closure(fields, ocean_cells, weights, forcing):
    weight_in, bias_in, weight_mid, bias_mid, weight_out, bias_out = weights
    columns = fields.reshape(weight_in.shape[0], -1)
    hidden = jnp.tanh(jnp.dot(weight_in.T, columns, precision=HIGHEST) + bias_in[:, None])
    hidden = jnp.tanh(jnp.dot(weight_mid.T, hidden, precision=HIGHEST) + bias_mid[:, None])
    output = (jnp.dot(weight_out.T, hidden, precision=HIGHEST) + bias_out[:, None]).reshape(fields.shape)
    output = output.at[1, 0].add(forcing)
    return ocean_cells * output

def reference(initial_state, land_mask, surface_flux, weight_in, bias_in, weight_mid, bias_mid, weight_out, bias_out, cotangent):
    ocean_cells = land_mask.astype(jnp.float32)
    top_ocean = ocean_cells[0]
    mean_flux = jnp.sum(top_ocean * surface_flux) / jnp.sum(top_ocean)
    forcing = -FRESHWATER * (surface_flux - mean_flux)
    inv_cos, coriolis = latitude_terms(jnp.arange(NLAT, dtype=jnp.float32), NLAT)

    def one_step(fields, weights):
        advanced = three_sections(fields, ocean_cells, inv_cos, coriolis)
        return advanced + TIME_STEP * closure(fields, ocean_cells, weights, forcing)
    stepper = jax.checkpoint(one_step)

    def run(source, weights):
        fields = ocean_cells * source
        for step_index in range(STEPS):
            fields = stepper(fields, weights)
        return fields
    weights = (weight_in, bias_in, weight_mid, bias_mid, weight_out, bias_out)
    final_state, pullback = jax.vjp(run, initial_state, weights)
    state_grad, weight_grads = pullback(cotangent)
    grad_scale = 1.0 / math.sqrt(NLAT * NLON)
    return (final_state, state_grad, weight_grads[0] * grad_scale, weight_grads[1] * grad_scale, weight_grads[2] * grad_scale, weight_grads[3] * grad_scale, weight_grads[4] * grad_scale, weight_grads[5] * grad_scale)
```

```python
import functools
import math

import jax
import jax.numpy as jnp
from jax import lax
from jax.experimental import pallas as pl
from jax.experimental.pallas import tpu as pltpu
from jax.sharding import PartitionSpec as P

F32 = jnp.float32
BF16 = jnp.bfloat16
MESH = pl.DeviceIdType.MESH

LEV = 10
FEAT = 40
HID = 64
ROWS = 16
COLS = 128
CELLS = ROWS * COLS
PAD = 32

LAT_LIMIT = 1.2
DT = 0.25
MIX = (0.1, 0.1, 0.15, 0.15)
GAIN_S = 0.5 * 0.8
GAIN_T = -0.5 * 0.2
FRESHWATER = 2.0
CHUNK = 512


def split(x):
    hi = x.astype(BF16)
    lo = (x - hi.astype(F32)).astype(BF16)
    return hi, lo


def kernel(
    lat_count,
    lon_count,
    state,
    mask,
    flux,
    win,
    b_in,
    wmid,
    b_mid,
    wout,
    b_out,
    cot,
    fin,
    grad,
    g_win,
    g_bin,
    g_wmid,
    g_bmid,
    g_wout,
    g_bout,
    xs,
    ew,
    ns,
    pe,
    mw,
    pn,
    mn,
    acc,
    lam,
    t2,
    t1,
    zc,
    h1,
    h2,
    dout,
    da2,
    da1,
    mx,
    dx,
    dox,
    lhs,
    bcol,
    square,
    gb,
    rs1,
    c1,
    rs2,
    c2,
    ag,
    f0,
    fr1,
    f1,
    fr2,
    row_s,
    row_r,
    col_s,
    col_r,
    h_send,
    h_recv,
    a_send,
    a_recv,
):
    lon = lax.axis_index("lon")
    lat = lax.axis_index("lat")
    east = lax.rem(lon + 1, lon_count)
    west = lax.rem(lon + lon_count - 1, lon_count)
    has_n = lat < lat_count - 1
    has_s = lat > 0
    halves = 2
    near = lon_count // halves
    far = lat_count * halves
    share = 128 // near
    half = lon // near
    spot = lon - half * near
    other = lat * halves + half

    def along(d):
        return {"lon": half * near + lax.rem(spot + d, near), "lat": lat}

    def across(d):
        to = lax.rem(other + d, far)
        to_lat = to // halves
        return {"lon": (to - to_lat * halves) * near + spot, "lat": to_lat}

    north_id = {"lon": lon, "lat": lat + 1}
    south_id = {"lon": lon, "lat": lat - 1}
    east_id = {"lon": east, "lat": lat}
    west_id = {"lon": west, "lat": lat}

    barrier = pltpu.get_barrier_semaphore()

    def greet(to):
        pl.semaphore_signal(barrier, inc=1, device_id=to, device_id_type=MESH)

    greet(east_id)
    greet(west_id)

    @pl.when(has_n)
    def _():
        greet(north_id)

    @pl.when(has_s)
    def _():
        greet(south_id)

    for d in range(1, near):
        greet(along(d))
    for d in range(1, far):
        greet(across(d))

    lane = lax.broadcasted_iota(jnp.int32, (ROWS, COLS), 1)
    row = lax.broadcasted_iota(jnp.int32, (ROWS, COLS), 0)
    first_lane = lane == 0
    last_lane = lane == COLS - 1
    odd_lane = lax.rem(lane, 2) == 1
    low_lane = lane < 64
    grow = (row + lat * ROWS).astype(F32)
    phi = LAT_LIMIT * (2.0 * (grow + 0.5) / (lat_count * ROWS) - 1.0)
    sq = phi * phi
    cosine = jnp.ones_like(phi)
    sine = jnp.ones_like(phi)
    for n in range(8, 0, -1):
        cosine = 1.0 - cosine * sq * (1.0 / ((2 * n - 1) * (2 * n)))
        sine = 1.0 - sine * sq * (1.0 / ((2 * n) * (2 * n + 1)))
    inv_cos = 1.0 / cosine
    cor = sine * phi
    hm = 0.5 * inv_cos
    cc = inv_cos * inv_cos
    depth = mask[0]
    for l in range(1, LEV):
        depth = depth + mask[l]

    def hcopy(e, d):
        if d == 0:
            src, dst, to = row_s.at[e, 0], row_r.at[e, 0], north_id
        elif d == 1:
            src, dst, to = row_s.at[e, 1], row_r.at[e, 1], south_id
        elif d == 2:
            src, dst, to = col_s.at[e], col_r.at[e, 0], east_id
        else:
            src, dst, to = col_s.at[e], col_r.at[e, 1], west_id
        return pltpu.make_async_remote_copy(
            src_ref=src,
            dst_ref=dst,
            send_sem=h_send.at[e, d],
            recv_sem=h_recv.at[e, d],
            device_id=to,
            device_id_type=MESH,
        )

    def launch(e):
        @pl.when(has_n)
        def _():
            hcopy(e, 0).start()

        @pl.when(has_s)
        def _():
            hcopy(e, 1).start()

        hcopy(e, 2).start()
        hcopy(e, 3).start()

    def arrive(e):
        @pl.when(has_s)
        def _():
            hcopy(e, 0).wait_recv()

        @pl.when(has_n)
        def _():
            hcopy(e, 1).wait_recv()

        hcopy(e, 2).wait_recv()
        hcopy(e, 3).wait_recv()

    def drain(e):
        @pl.when(has_n)
        def _():
            hcopy(e, 0).wait_send()

        @pl.when(has_s)
        def _():
            hcopy(e, 1).wait_send()

        hcopy(e, 2).wait_send()
        hcopy(e, 3).wait_send()

    def take_rows(ref, r, count):
        return ref.reshape(FEAT * count, COLS)[pl.ds(r, FEAT, stride=count), :]

    def put_rows(ref, r, count, value):
        ref.reshape(FEAT * count, COLS)[pl.ds(r, FEAT, stride=count), :] = value

    def pack(packed, value, fl):
        turned = pltpu.roll(value, 2 * fl + 1, 1)
        return jnp.where(lane // 2 == fl, turned, packed)

    def part(at):
        return pl.ds(pl.multiple_of(at * share, share), share)

    def others(stage):
        return range(1, far if stage in (1, 3) else near)

    def fan(stage, d, src, dst, to):
        return pltpu.make_async_remote_copy(
            src_ref=src,
            dst_ref=dst,
            send_sem=a_send.at[stage, d],
            recv_sem=a_recv.at[stage, d],
            device_id=to,
            device_id_type=MESH,
        )

    def fan_copy(stage, d):
        if stage == 0:
            return fan(stage, d, f0, fr1.at[d], along(d))
        if stage == 1:
            return fan(stage, d, f1, fr2.at[d], across(d))
        if stage == 2:
            return fan(stage, d, gb.at[part(lax.rem(spot + d, near))], rs1.at[d], along(d))
        if stage == 3:
            return fan(stage, d, c1, rs2.at[d], across(d))
        return fan(stage, d, c2, ag.at[part(spot)], along(d))

    def fan_start(stage):
        for d in others(stage):
            fan_copy(stage, d).start()

    def fan_arrive(stage):
        for d in others(stage):
            fan_copy(stage, d).wait_recv()

    def fan_drain(stage):
        for d in others(stage):
            fan_copy(stage, d).wait_send()

    def slot_sum(stage, own, slots):
        total = own
        for d in others(stage):
            total = total + slots[d]
        return total

    def begin(l, packed):
        wet = depth > l
        for f in range(4):
            fl = f * LEV + l
            x = jnp.where(wet, state[fl], 0.0)
            xs[0, fl, 8:24, :] = x
            packed = pack(packed, x, fl)
        return packed

    blank = jnp.zeros((ROWS, COLS), F32)
    packed = lax.fori_loop(0, LEV, begin, blank)
    col_s[0] = packed

    def stage_rows(e, north_ref, south_ref):
        row_s[e, 0] = take_rows(north_ref, 23, PAD)
        row_s[e, 1] = take_rows(south_ref, 8, PAD)

    stage_rows(0, xs.at[0], xs.at[0])
    wet_top = depth > 0
    part_flux = jnp.sum(jnp.where(wet_top, flux[...], 0.0), axis=0, keepdims=True)
    part_count = jnp.sum(jnp.where(wet_top, 1.0, 0.0), axis=0, keepdims=True)
    row8 = lax.broadcasted_iota(jnp.int32, (8, COLS), 0)
    f0[...] = jnp.where(
        row8 == 0,
        jnp.broadcast_to(part_flux, (8, COLS)),
        jnp.where(row8 == 1, jnp.broadcast_to(part_count, (8, COLS)), 0.0),
    )

    meet = near + far + has_n.astype(jnp.int32) + has_s.astype(jnp.int32)
    pl.semaphore_wait(barrier, meet)
    launch(0)
    fan_start(0)

    @pl.when(jnp.logical_not(has_s))
    def _():
        for e in range(12):
            row_r[e, 0] = jnp.zeros((FEAT, COLS), F32)

    @pl.when(jnp.logical_not(has_n))
    def _():
        for e in range(12):
            row_r[e, 1] = jnp.zeros((FEAT, COLS), F32)

    def weight(at, value):
        hi, lo = split(value)
        lhs[at, :, 0:64] = hi
        lhs[at, :, 64:128] = hi
        lhs[at, :, 128:192] = lo

    def both(value_ref, rows, cols, plain, turned):
        square[...] = jnp.zeros((COLS, COLS), F32)
        square[0:rows, 0:cols] = value_ref[...]
        whole = square[...]
        weight(plain, whole[0:64, 0:64])
        weight(turned, whole.T[0:64, 0:64])

    def prepare():
        both(wout, HID, FEAT, 3, 2)
        both(wmid, HID, HID, 4, 1)
        both(win, FEAT, HID, 5, 0)
        square[...] = jnp.zeros((COLS, COLS), F32)
        square[0:1, 0:HID] = b_in[...]
        square[1:2, 0:HID] = b_mid[...]
        square[2:3, 0:FEAT] = b_out[...]
        turned = square[...].T
        for at in range(3):
            bcol[at] = jnp.broadcast_to(turned[0:64, at : at + 1], (64, COLS))
        for s in range(2):
            zc[s, FEAT:64, :] = jnp.zeros((64 - FEAT, CELLS), F32)
        dout[FEAT:64, :] = jnp.zeros((64 - FEAT, CELLS), F32)
        gb[112:128] = jnp.zeros((16, COLS), F32)

    def product(at, x):
        hi, lo = split(x)
        return jnp.dot(
            lhs[at], jnp.concatenate([hi, lo, hi], axis=0), preferred_element_type=F32
        )

    def bias(at):
        return jnp.concatenate([bcol[at]] * (CHUNK // COLS), axis=1)

    def gather(ref, first, count, out):
        for r in range(ROWS):
            out[0:FEAT, r * COLS : (r + 1) * COLS] = take_rows(ref, first + r, count)

    chunks = [pl.ds(c * CHUNK, CHUNK) for c in range(CELLS // CHUNK)]

    def layer_one(s):
        gather(xs.at[3 * s], 8, PAD, zc.at[s])
        for c in chunks:
            h1[s, :, c] = jnp.tanh(product(0, zc[s, :, c]) + bias(0))

    def layer_two(s):
        for c in chunks:
            h2[s, :, c] = jnp.tanh(product(1, h1[s, :, c]) + bias(1))

    def scatter(ref, n, value):
        for j in range(CHUNK // COLS):
            put_rows(
                ref, n * (CHUNK // COLS) + j, ROWS, value[0:FEAT, j * COLS : (j + 1) * COLS]
            )

    def layer_three(s):
        for n, c in enumerate(chunks):
            scatter(mx, n, product(2, h2[s, :, c]) + bias(2))

    def back_out(s, source):
        def body(l, carry):
            wet = depth > l
            for f in range(4):
                fl = f * LEV + l
                dox[fl] = jnp.where(wet, DT * source[fl], 0.0)
            return carry

        lax.fori_loop(0, LEV, body, 0)
        gather(dox, 0, ROWS, dout)
        for c in chunks:
            h = h2[s, :, c]
            da2[:, c] = product(3, dout[:, c]) * (1.0 - h * h)

    def back_mid(s):
        for c in chunks:
            h = h1[s, :, c]
            da1[:, c] = product(4, da2[:, c]) * (1.0 - h * h)

    def back_in(s):
        for n, c in enumerate(chunks):
            scatter(dx, n, product(5, da1[:, c]))

    def outer(left_ref, right_ref):
        total = jnp.zeros((144, COLS), F32)
        ones = jnp.ones((16, CHUNK), BF16)
        for c in chunks:
            hi, lo = split(left_ref[:, c])
            r_hi, r_lo = split(right_ref[:, c])
            total = total + lax.dot_general(
                jnp.concatenate([hi, lo, ones], axis=0),
                jnp.concatenate([r_hi, r_lo], axis=0),
                (((1,), (1,)), ((), ())),
                preferred_element_type=F32,
            )
        folded = total + pltpu.roll(total, 64, 1)
        return folded[0:64] + total[64:128], folded[128:136]

    def weight_grads(s, add):
        g_in, s_in = outer(zc.at[s], da1)
        g_mid, s_mid = outer(h1.at[s], da2)
        g_out, s_out = outer(h2.at[s], dout)
        wide = lax.broadcasted_iota(jnp.int32, (64, COLS), 1) < 64
        low8 = lax.broadcasted_iota(jnp.int32, (8, COLS), 1) < 64
        top = jnp.where(wide, g_mid, pltpu.roll(g_out, 64, 1))
        low = jnp.where(wide, g_in, 0.0)[0:FEAT]
        sums = jnp.where(
            row8 == 0, s_in, jnp.where(row8 == 1, s_mid, jnp.where(row8 == 2, s_out, 0.0))
        )
        sums = jnp.where(low8, sums, 0.0)
        if add:
            gb[0:64] = gb[0:64] + top
            gb[64:104] = gb[64:104] + low
            gb[104:112] = gb[104:112] + sums
        else:
            gb[0:64] = top
            gb[64:104] = low
            gb[104:112] = sums

    def sides(turned, q_west, q_east):
        w_side = pltpu.roll(jnp.where(last_lane, turned, q_west), 1, 1)
        e_side = pltpu.roll(jnp.where(first_lane, turned, q_east), COLS - 1, 1)
        return w_side, e_side

    def halo(e):
        return jnp.where(odd_lane, col_r[e, 1], col_r[e, 0])

    def turn(packed, fl):
        return pltpu.roll(packed, lax.rem(2 * COLS - 1 - 2 * fl, COLS), 1)

    def forward(k, forcing):
        start, stage = 3 * (k // 3), k % 3
        arrive(k)
        put_rows(xs.at[k], 7, PAD, row_r[k, 0])
        put_rows(xs.at[k], 24, PAD, row_r[k, 1])
        received = halo(k)

        def body(l, carry):
            packed, press_x, press_y = carry
            wet = depth > l
            u = xs[k, 2 * LEV + l, 8:24, :]
            v = xs[k, 3 * LEV + l, 8:24, :]
            uh = u * hm
            vh = v * 0.5
            for f in range(4):
                fl = f * LEV + l
                q = xs[k, fl, 8:24, :]
                north = xs[k, fl, 9:25, :]
                south = xs[k, fl, 7:23, :]
                w_side, e_side = sides(turn(received, fl), q, q)
                d_x = e_side - w_side
                d_y = north - south
                ew[k, fl] = d_x
                ns[k, fl] = d_y
                mix = MIX[f]
                change = (
                    (mix * cc) * (e_side + w_side - 2.0 * q)
                    + mix * (north + south - 2.0 * q)
                    - (uh * d_x + vh * d_y)
                )
                if f == 0:
                    press_x = press_x + GAIN_T * d_x
                    press_y = press_y + GAIN_T * d_y
                if f == 1:
                    press_x = press_x + GAIN_S * d_x
                    press_y = press_y + GAIN_S * d_y
                if f == 2:
                    change = change + (cor * v - press_x * hm)
                if f == 3:
                    change = change - (cor * u + press_y * 0.5)
                moved = q + jnp.where(wet, DT * change, 0.0)
                if stage == 0:
                    new = moved
                elif stage == 1:
                    new = 0.75 * xs[start, fl, 8:24, :] + 0.25 * moved
                else:
                    given = mx[fl]
                    if f == 1:
                        given = given + jnp.where(l == 0, forcing, 0.0)
                    new = (
                        (1.0 / 3.0) * xs[start, fl, 8:24, :]
                        + (2.0 / 3.0) * moved
                        + jnp.where(wet, DT * given, 0.0)
                    )
                if k < 5:
                    xs[k + 1, fl, 8:24, :] = new
                    packed = pack(packed, new, fl)
                else:
                    fin[fl] = new
            return packed, press_x, press_y

        packed, _, _ = lax.fori_loop(0, LEV, body, (blank, blank, blank))
        if k < 5:
            col_s[k + 1] = packed
            stage_rows(k + 1, xs.at[k + 1], xs.at[k + 1])
            launch(k + 1)

    def give(n, source):
        k, stage = 5 - n, (5 - n) % 3
        scale = (1.0, 0.25, 2.0 / 3.0)[stage]

        def body(t, carry):
            packed, sum_u, sum_v = carry
            l = LEV - 1 - t
            wet = depth > l
            g = [jnp.where(wet, (DT * scale) * source[f * LEV + l], 0.0) for f in range(4)]
            sum_u = sum_u + g[2]
            sum_v = sum_v + g[3]
            u = xs[k, 2 * LEV + l, 8:24, :]
            v = xs[k, 3 * LEV + l, 8:24, :]
            uh = u * hm
            vh = v * 0.5
            push_x = hm * sum_u
            push_y = 0.5 * sum_v
            to_u = cor * g[3]
            to_v = cor * g[2]
            for f in range(4):
                fl = f * LEV + l
                mix = MIX[f]
                a = uh * g[f]
                b = vh * g[f]
                if f == 0:
                    a = a + GAIN_T * push_x
                    b = b + GAIN_T * push_y
                if f == 1:
                    a = a + GAIN_S * push_x
                    b = b + GAIN_S * push_y
                base = (mix * cc) * g[f]
                plus = base + a
                minus = base - a
                flat = mix * g[f]
                pe[fl] = plus
                mw[fl] = minus
                pn[fl, 8:24, :] = flat + b
                mn[fl, 8:24, :] = flat - b
                packed = pack(packed, jnp.where(low_lane, plus, minus), fl)
                to_u = to_u + g[f] * (hm * ew[k, fl])
                to_v = to_v - g[f] * (0.5 * ns[k, fl])
            for f in range(4):
                fl = f * LEV + l
                own = -2.0 * (MIX[f] * cc + MIX[f]) * g[f]
                if f == 2:
                    own = own - to_u
                if f == 3:
                    own = own + to_v
                acc[fl] = own
            return packed, sum_u, sum_v

        packed, _, _ = lax.fori_loop(0, LEV, body, (blank, blank, blank))
        col_s[6 + n] = packed
        stage_rows(6 + n, mn, pn)
        launch(6 + n)

    def take(n, source):
        stage = (5 - n) % 3
        e = 6 + n
        arrive(e)
        put_rows(mn, 7, PAD, row_r[e, 0])
        put_rows(pn, 24, PAD, row_r[e, 1])
        received = halo(e)

        def body(l, carry):
            for f in range(4):
                fl = f * LEV + l
                w_side, e_side = sides(turn(received, fl), mw[fl], pe[fl])
                got = acc[fl] + w_side + e_side + pn[fl, 9:25, :] + mn[fl, 7:23, :]
                if stage == 2:
                    t2[fl] = (2.0 / 3.0) * source[fl] + got
                elif stage == 1:
                    t1[fl] = 0.25 * t2[fl] + got
                else:
                    new = (1.0 / 3.0) * source[fl] + 0.75 * t2[fl] + t1[fl] + got + dx[fl]
                    if n == 5:
                        grad[fl] = jnp.where(depth > l, new, 0.0)
                    else:
                        lam[fl] = new
            return carry

        lax.fori_loop(0, LEV, body, 0)

    prepare()
    layer_one(0)
    forward(0, None)
    fan_arrive(0)
    f1[...] = slot_sum(0, f0[...], fr1)
    fan_start(1)
    layer_two(0)
    forward(1, None)
    layer_three(0)
    fan_arrive(1)
    totals = slot_sum(1, f1[...], fr2)
    flux_sum = jnp.sum(totals[0:1, :], axis=1, keepdims=True)
    count_sum = jnp.sum(totals[1:2, :], axis=1, keepdims=True)
    mean = jnp.broadcast_to(flux_sum / count_sum, (ROWS, COLS))
    forcing = -FRESHWATER * (flux[...] - mean)
    forward(2, forcing)
    layer_one(1)
    forward(3, None)
    layer_two(1)
    forward(4, None)
    layer_three(1)
    forward(5, forcing)

    give(0, cot)
    back_out(1, cot)
    take(0, cot)
    give(1, t2)
    back_mid(1)
    back_in(1)
    take(1, cot)
    give(2, t1)
    weight_grads(1, False)
    take(2, cot)
    give(3, lam)
    back_out(0, lam)
    back_mid(0)
    take(3, lam)
    give(4, t2)
    weight_grads(0, True)
    fan_start(2)
    back_in(0)
    take(4, lam)
    give(5, t1)
    fan_arrive(2)
    c1[...] = slot_sum(2, gb[part(spot)], rs1)
    fan_start(3)
    take(5, lam)
    fan_arrive(3)
    scale = 1.0 / math.sqrt(lat_count * ROWS * lon_count * COLS)
    c2[...] = slot_sum(3, c1[...], rs2) * scale
    ag[part(spot)] = c2[...]
    fan_start(4)
    for e in range(12):
        drain(e)
    for stage in range(4):
        fan_drain(stage)
    fan_arrive(4)
    top = ag[0:64]
    g_wmid[...] = top[:, 0:HID]
    g_wout[...] = pltpu.roll(top, 64, 1)[:, 0:FEAT]
    g_win[...] = ag[64:104][:, 0:HID]
    sums = ag[104:112]
    g_bin[...] = sums[0:1, 0:HID]
    g_bmid[...] = sums[1:2, 0:HID]
    g_bout[...] = sums[2:3, 0:FEAT]
    fan_drain(4)


def on_device(lat_count, lon_count, state, mask, flux, win, b_in, wmid, b_mid, wout, b_out, cot):
    def v(*shape):
        return pltpu.VMEM(shape, F32)

    near, far = lon_count // 2, lat_count * 2
    share = 128 // near
    vmem = pl.BlockSpec(memory_space=pltpu.VMEM)
    field = (FEAT, ROWS, COLS)
    tall = (FEAT, PAD, COLS)
    wide = (64, CELLS)
    out = pl.pallas_call(
        functools.partial(kernel, lat_count, lon_count),
        out_shape=[
            jax.ShapeDtypeStruct(shape, F32)
            for shape in (
                field,
                field,
                (FEAT, HID),
                (1, HID),
                (HID, HID),
                (1, HID),
                (HID, FEAT),
                (1, FEAT),
            )
        ],
        in_specs=[vmem] * 10,
        out_specs=[vmem] * 8,
        scratch_shapes=[
            v(6, *tall),
            v(6, *field),
            v(6, *field),
            v(*field),
            v(*field),
            v(*tall),
            v(*tall),
            v(*field),
            v(*field),
            v(*field),
            v(*field),
            v(2, *wide),
            v(2, *wide),
            v(2, *wide),
            v(*wide),
            v(*wide),
            v(*wide),
            v(*field),
            v(*field),
            v(*field),
            pltpu.VMEM((6, 64, 192), BF16),
            v(3, 64, COLS),
            v(COLS, COLS),
            v(128, COLS),
            v(near, share, COLS),
            v(share, COLS),
            v(far, share, COLS),
            v(share, COLS),
            v(128, COLS),
            v(8, COLS),
            v(near, 8, COLS),
            v(8, COLS),
            v(far, 8, COLS),
            v(12, 2, FEAT, COLS),
            v(12, 2, FEAT, COLS),
            v(12, ROWS, COLS),
            v(12, 2, ROWS, COLS),
            pltpu.SemaphoreType.DMA((12, 4)),
            pltpu.SemaphoreType.DMA((12, 4)),
            pltpu.SemaphoreType.DMA((5, max(near, far))),
            pltpu.SemaphoreType.DMA((5, max(near, far))),
        ],
        compiler_params=pltpu.CompilerParams(
            collective_id=0, has_side_effects=True, vmem_limit_bytes=60 * 1024 * 1024
        ),
    )(
        state.reshape(field),
        mask,
        flux,
        win,
        b_in.reshape(1, HID),
        wmid,
        b_mid.reshape(1, HID),
        wout,
        b_out.reshape(1, FEAT),
        cot.reshape(field),
    )
    shape4 = (4, LEV, ROWS, COLS)
    return (
        out[0].reshape(shape4),
        out[1].reshape(shape4),
        out[2],
        out[3].reshape(HID),
        out[4],
        out[5].reshape(HID),
        out[6],
        out[7].reshape(FEAT),
    )


def solution(mesh):
    block = P(None, None, "lat", "lon")
    return jax.shard_map(
        functools.partial(on_device, mesh.shape["lat"], mesh.shape["lon"]),
        mesh=mesh,
        in_specs=(
            block,
            P(None, "lat", "lon"),
            P("lat", "lon"),
            P(),
            P(),
            P(),
            P(),
            P(),
            P(),
            block,
        ),
        out_specs=(block, block, P(), P(), P(), P(), P(), P()),
        check_vma=False,
    )
```

```python
import functools
import math

import jax
import jax.numpy as jnp
from jax import lax
from jax.experimental import pallas as pl
from jax.experimental.pallas import tpu as pltpu
from jax.sharding import PartitionSpec as P

F32 = jnp.float32
BF16 = jnp.bfloat16
MESH = pl.DeviceIdType.MESH

LEV = 10
FEAT = 40
HID = 64
ROWS = 16
COLS = 128
CELLS = ROWS * COLS
PAD = 32

LAT_LIMIT = 1.2
DT = 0.25
MIX = (0.1, 0.1, 0.15, 0.15)
GAIN_S = 0.5 * 0.8
GAIN_T = -0.5 * 0.2
FRESHWATER = 2.0
CHUNK = 512


def split(x):
    hi = x.astype(BF16)
    lo = (x - hi.astype(F32)).astype(BF16)
    return hi, lo


def kernel(
    lat_count,
    lon_count,
    state,
    mask,
    flux,
    win,
    b_in,
    wmid,
    b_mid,
    wout,
    b_out,
    cot,
    fin,
    grad,
    ag,
    xs,
    ew,
    ns,
    pe,
    mw,
    pn,
    mn,
    acc,
    lam,
    t2,
    t1,
    zc,
    h1,
    h2,
    dout,
    da2,
    da1,
    mx,
    dx,
    dox,
    lhs,
    bcol,
    square,
    gb,
    rs1,
    c1,
    rs2,
    c2,
    f0,
    fr1,
    f1,
    fr2,
    row_s,
    row_r,
    col_s,
    col_r,
    h_send,
    h_recv,
    a_send,
    a_recv,
):
    lon = lax.axis_index("lon")
    lat = lax.axis_index("lat")
    east = lax.rem(lon + 1, lon_count)
    west = lax.rem(lon + lon_count - 1, lon_count)
    has_n = lat < lat_count - 1
    has_s = lat > 0
    halves = 2
    near = lon_count // halves
    far = lat_count * halves
    share = 128 // near
    half = lon // near
    spot = lon - half * near
    other = lat * halves + half

    def along(d):
        return {"lon": half * near + lax.rem(spot + d, near), "lat": lat}

    def across(d):
        to = lax.rem(other + d, far)
        to_lat = to // halves
        return {"lon": (to - to_lat * halves) * near + spot, "lat": to_lat}

    north_id = {"lon": lon, "lat": lat + 1}
    south_id = {"lon": lon, "lat": lat - 1}
    east_id = {"lon": east, "lat": lat}
    west_id = {"lon": west, "lat": lat}

    barrier = pltpu.get_barrier_semaphore()

    def greet(to):
        pl.semaphore_signal(barrier, inc=1, device_id=to, device_id_type=MESH)

    greet(east_id)
    greet(west_id)

    @pl.when(has_n)
    def _():
        greet(north_id)

    @pl.when(has_s)
    def _():
        greet(south_id)

    for d in range(1, near):
        greet(along(d))
    for d in range(1, far):
        greet(across(d))

    lane = lax.broadcasted_iota(jnp.int32, (ROWS, COLS), 1)
    row = lax.broadcasted_iota(jnp.int32, (ROWS, COLS), 0)
    first_lane = lane == 0
    last_lane = lane == COLS - 1
    odd_lane = lax.rem(lane, 2) == 1
    low_lane = lane < 64
    grow = (row + lat * ROWS).astype(F32)
    phi = LAT_LIMIT * (2.0 * (grow + 0.5) / (lat_count * ROWS) - 1.0)
    sq = phi * phi
    cosine = jnp.ones_like(phi)
    sine = jnp.ones_like(phi)
    for n in range(8, 0, -1):
        cosine = 1.0 - cosine * sq * (1.0 / ((2 * n - 1) * (2 * n)))
        sine = 1.0 - sine * sq * (1.0 / ((2 * n) * (2 * n + 1)))
    inv_cos = 1.0 / cosine
    cor = sine * phi
    hm = 0.5 * inv_cos
    cc = inv_cos * inv_cos
    depth = mask[0]
    for l in range(1, LEV):
        depth = depth + mask[l]

    def hcopy(e, d):
        if d == 0:
            src, dst, to = row_s.at[e, 0], row_r.at[e, 0], north_id
        elif d == 1:
            src, dst, to = row_s.at[e, 1], row_r.at[e, 1], south_id
        elif d == 2:
            src, dst, to = col_s.at[e], col_r.at[e, 0], east_id
        else:
            src, dst, to = col_s.at[e], col_r.at[e, 1], west_id
        return pltpu.make_async_remote_copy(
            src_ref=src,
            dst_ref=dst,
            send_sem=h_send.at[e, d],
            recv_sem=h_recv.at[e, d],
            device_id=to,
            device_id_type=MESH,
        )

    def launch(e):
        @pl.when(has_n)
        def _():
            hcopy(e, 0).start()

        @pl.when(has_s)
        def _():
            hcopy(e, 1).start()

        hcopy(e, 2).start()
        hcopy(e, 3).start()

    def arrive(e):
        @pl.when(has_s)
        def _():
            hcopy(e, 0).wait_recv()

        @pl.when(has_n)
        def _():
            hcopy(e, 1).wait_recv()

        hcopy(e, 2).wait_recv()
        hcopy(e, 3).wait_recv()

    def drain(e):
        @pl.when(has_n)
        def _():
            hcopy(e, 0).wait_send()

        @pl.when(has_s)
        def _():
            hcopy(e, 1).wait_send()

        hcopy(e, 2).wait_send()
        hcopy(e, 3).wait_send()

    def take_rows(ref, r, count):
        return ref.reshape(FEAT * count, COLS)[pl.ds(r, FEAT, stride=count), :]

    def put_rows(ref, r, count, value):
        ref.reshape(FEAT * count, COLS)[pl.ds(r, FEAT, stride=count), :] = value

    def pack(packed, value, fl):
        turned = pltpu.roll(value, 2 * fl + 1, 1)
        return jnp.where(lane // 2 == fl, turned, packed)

    def part(at):
        return pl.ds(pl.multiple_of(at * share, share), share)

    def others(stage):
        return range(1, far if stage in (1, 3) else near)

    def fan(stage, d, src, dst, to):
        return pltpu.make_async_remote_copy(
            src_ref=src,
            dst_ref=dst,
            send_sem=a_send.at[stage, d],
            recv_sem=a_recv.at[stage, d],
            device_id=to,
            device_id_type=MESH,
        )

    def fan_copy(stage, d):
        if stage == 0:
            return fan(stage, d, f0, fr1.at[d], along(d))
        if stage == 1:
            return fan(stage, d, f1, fr2.at[d], across(d))
        if stage == 2:
            return fan(stage, d, gb.at[part(lax.rem(spot + d, near))], rs1.at[d], along(d))
        if stage == 3:
            return fan(stage, d, c1, rs2.at[d], across(d))
        return fan(stage, d, c2, ag.at[part(spot)], along(d))

    def fan_start(stage):
        for d in others(stage):
            fan_copy(stage, d).start()

    def fan_arrive(stage):
        for d in others(stage):
            fan_copy(stage, d).wait_recv()

    def fan_drain(stage):
        for d in others(stage):
            fan_copy(stage, d).wait_send()

    def slot_sum(stage, own, slots):
        total = own
        for d in others(stage):
            total = total + slots[d]
        return total

    def levels(body, carry):
        for l in range(LEV):
            carry = body(l, carry)
        return carry

    def begin(l, packed):
        wet = depth > l
        for f in range(4):
            fl = f * LEV + l
            x = jnp.where(wet, state[fl], 0.0)
            xs[0, fl, 8:24, :] = x
            packed = pack(packed, x, fl)
        return packed

    blank = jnp.zeros((ROWS, COLS), F32)
    packed = levels(begin, blank)
    col_s[0] = packed

    def stage_rows(e, north_ref, south_ref):
        row_s[e, 0] = take_rows(north_ref, 23, PAD)
        row_s[e, 1] = take_rows(south_ref, 8, PAD)

    stage_rows(0, xs.at[0], xs.at[0])
    wet_top = depth > 0
    part_flux = jnp.sum(jnp.where(wet_top, flux[...], 0.0), axis=0, keepdims=True)
    part_count = jnp.sum(jnp.where(wet_top, 1.0, 0.0), axis=0, keepdims=True)
    row8 = lax.broadcasted_iota(jnp.int32, (8, COLS), 0)
    f0[...] = jnp.where(
        row8 == 0,
        jnp.broadcast_to(part_flux, (8, COLS)),
        jnp.where(row8 == 1, jnp.broadcast_to(part_count, (8, COLS)), 0.0),
    )

    meet = near + far + has_n.astype(jnp.int32) + has_s.astype(jnp.int32)
    pl.semaphore_wait(barrier, meet)
    launch(0)
    fan_start(0)

    @pl.when(jnp.logical_not(has_s))
    def _():
        for e in range(12):
            row_r[e, 0] = jnp.zeros((FEAT, COLS), F32)

    @pl.when(jnp.logical_not(has_n))
    def _():
        for e in range(12):
            row_r[e, 1] = jnp.zeros((FEAT, COLS), F32)

    def weight(at, value):
        hi, lo = split(value)
        lhs[at, :, 0:64] = hi
        lhs[at, :, 64:128] = hi
        lhs[at, :, 128:192] = lo

    def both(value_ref, rows, cols, plain, turned):
        square[...] = jnp.zeros((COLS, COLS), F32)
        square[0:rows, 0:cols] = value_ref[...]
        whole = square[...]
        weight(plain, whole[0:64, 0:64])
        weight(turned, whole.T[0:64, 0:64])

    def prepare():
        both(wout, FEAT, HID, 2, 3)
        both(wmid, HID, HID, 4, 1)
        both(win, FEAT, HID, 5, 0)
        square[...] = jnp.zeros((COLS, COLS), F32)
        square[0:1, 0:HID] = b_in[...]
        square[1:2, 0:HID] = b_mid[...]
        square[2:3, 0:FEAT] = b_out[...]
        turned = square[...].T
        for at in range(3):
            bcol[at] = jnp.broadcast_to(turned[0:64, at : at + 1], (64, COLS))
        for s in range(2):
            zc[s, FEAT:64, :] = jnp.zeros((64 - FEAT, CELLS), F32)
        dout[FEAT:64, :] = jnp.zeros((64 - FEAT, CELLS), F32)
        gb[112:128] = jnp.zeros((16, COLS), F32)

    def product(at, x):
        hi, lo = split(x)
        return jnp.dot(
            lhs[at], jnp.concatenate([hi, lo, hi], axis=0), preferred_element_type=F32
        )

    def bias(at):
        return jnp.concatenate([bcol[at]] * (CHUNK // COLS), axis=1)

    def gather(ref, first, count, out):
        for r in range(ROWS):
            out[0:FEAT, r * COLS : (r + 1) * COLS] = take_rows(ref, first + r, count)

    chunks = [pl.ds(c * CHUNK, CHUNK) for c in range(CELLS // CHUNK)]

    def layer_one(s):
        gather(xs.at[3 * s], 8, PAD, zc.at[s])
        for c in chunks:
            h1[s, :, c] = jnp.tanh(product(0, zc[s, :, c]) + bias(0))

    def layer_two(s):
        for c in chunks:
            h2[s, :, c] = jnp.tanh(product(1, h1[s, :, c]) + bias(1))

    def scatter(ref, n, value):
        for j in range(CHUNK // COLS):
            put_rows(
                ref, n * (CHUNK // COLS) + j, ROWS, value[0:FEAT, j * COLS : (j + 1) * COLS]
            )

    def layer_three(s):
        for n, c in enumerate(chunks):
            scatter(mx, n, product(2, h2[s, :, c]) + bias(2))

    def back_out(s, source):
        def body(l, carry):
            wet = depth > l
            for f in range(4):
                fl = f * LEV + l
                dox[fl] = jnp.where(wet, DT * source[fl], 0.0)
            return carry

        levels(body, 0)
        gather(dox, 0, ROWS, dout)
        for c in chunks:
            h = h2[s, :, c]
            da2[:, c] = product(3, dout[:, c]) * (1.0 - h * h)

    def back_mid(s):
        for c in chunks:
            h = h1[s, :, c]
            da1[:, c] = product(4, da2[:, c]) * (1.0 - h * h)

    def back_in(s):
        for n, c in enumerate(chunks):
            scatter(dx, n, product(5, da1[:, c]))

    def outer(left_ref, right_ref):
        total = jnp.zeros((144, COLS), F32)
        ones = jnp.ones((16, CHUNK), BF16)
        for c in chunks:
            hi, lo = split(left_ref[:, c])
            r_hi, r_lo = split(right_ref[:, c])
            total = total + lax.dot_general(
                jnp.concatenate([hi, lo, ones], axis=0),
                jnp.concatenate([r_hi, r_lo], axis=0),
                (((1,), (1,)), ((), ())),
                preferred_element_type=F32,
            )
        folded = total + pltpu.roll(total, 64, 1)
        return folded[0:64] + total[64:128], folded[128:136]

    def weight_grads(s, add):
        g_in, s_in = outer(zc.at[s], da1)
        g_mid, s_mid = outer(h1.at[s], da2)
        g_out, s_out = outer(h2.at[s], dout)
        wide = lax.broadcasted_iota(jnp.int32, (64, COLS), 1) < 64
        low8 = lax.broadcasted_iota(jnp.int32, (8, COLS), 1) < 64
        top = jnp.where(wide, g_mid, pltpu.roll(g_out, 64, 1))
        low = jnp.where(wide, g_in, 0.0)[0:FEAT]
        sums = jnp.where(
            row8 == 0, s_in, jnp.where(row8 == 1, s_mid, jnp.where(row8 == 2, s_out, 0.0))
        )
        sums = jnp.where(low8, sums, 0.0)
        if add:
            gb[0:64] = gb[0:64] + top
            gb[64:104] = gb[64:104] + low
            gb[104:112] = gb[104:112] + sums
        else:
            gb[0:64] = top
            gb[64:104] = low
            gb[104:112] = sums

    def sides(turned, q_west, q_east):
        w_side = pltpu.roll(jnp.where(last_lane, turned, q_west), 1, 1)
        e_side = pltpu.roll(jnp.where(first_lane, turned, q_east), COLS - 1, 1)
        return w_side, e_side

    def halo(e):
        return jnp.where(odd_lane, col_r[e, 1], col_r[e, 0])

    def turn(packed, fl):
        return pltpu.roll(packed, COLS - 1 - 2 * fl, 1)

    def forward(k, forcing):
        start, stage = 3 * (k // 3), k % 3
        arrive(k)
        put_rows(xs.at[k], 7, PAD, row_r[k, 0])
        put_rows(xs.at[k], 24, PAD, row_r[k, 1])
        received = halo(k)

        def body(l, carry):
            packed, press_x, press_y = carry
            wet = depth > l
            u = xs[k, 2 * LEV + l, 8:24, :]
            v = xs[k, 3 * LEV + l, 8:24, :]
            uh = u * hm
            vh = v * 0.5
            for f in range(4):
                fl = f * LEV + l
                q = xs[k, fl, 8:24, :]
                north = xs[k, fl, 9:25, :]
                south = xs[k, fl, 7:23, :]
                w_side, e_side = sides(turn(received, fl), q, q)
                d_x = e_side - w_side
                d_y = north - south
                ew[k, fl] = d_x
                ns[k, fl] = d_y
                mix = MIX[f]
                change = (
                    (mix * cc) * (e_side + w_side - 2.0 * q)
                    + mix * (north + south - 2.0 * q)
                    - (uh * d_x + vh * d_y)
                )
                if f == 0:
                    press_x = press_x + GAIN_T * d_x
                    press_y = press_y + GAIN_T * d_y
                if f == 1:
                    press_x = press_x + GAIN_S * d_x
                    press_y = press_y + GAIN_S * d_y
                if f == 2:
                    change = change + (cor * v - press_x * hm)
                if f == 3:
                    change = change - (cor * u + press_y * 0.5)
                moved = q + jnp.where(wet, DT * change, 0.0)
                if stage == 0:
                    new = moved
                elif stage == 1:
                    new = 0.75 * xs[start, fl, 8:24, :] + 0.25 * moved
                else:
                    given = mx[fl]
                    if f == 1 and l == 0:
                        given = given + forcing
                    new = (
                        (1.0 / 3.0) * xs[start, fl, 8:24, :]
                        + (2.0 / 3.0) * moved
                        + jnp.where(wet, DT * given, 0.0)
                    )
                if k < 5:
                    xs[k + 1, fl, 8:24, :] = new
                    packed = pack(packed, new, fl)
                else:
                    fin[fl] = new
            return packed, press_x, press_y

        packed, _, _ = levels(body, (blank, blank, blank))
        if k < 5:
            col_s[k + 1] = packed
            stage_rows(k + 1, xs.at[k + 1], xs.at[k + 1])
            launch(k + 1)

    def give(n, source):
        k, stage = 5 - n, (5 - n) % 3
        scale = (1.0, 0.25, 2.0 / 3.0)[stage]

        def body(t, carry):
            packed, sum_u, sum_v = carry
            l = LEV - 1 - t
            wet = depth > l
            g = [jnp.where(wet, (DT * scale) * source[f * LEV + l], 0.0) for f in range(4)]
            sum_u = sum_u + g[2]
            sum_v = sum_v + g[3]
            u = xs[k, 2 * LEV + l, 8:24, :]
            v = xs[k, 3 * LEV + l, 8:24, :]
            uh = u * hm
            vh = v * 0.5
            push_x = hm * sum_u
            push_y = 0.5 * sum_v
            to_u = cor * g[3]
            to_v = cor * g[2]
            for f in range(4):
                fl = f * LEV + l
                mix = MIX[f]
                a = uh * g[f]
                b = vh * g[f]
                if f == 0:
                    a = a + GAIN_T * push_x
                    b = b + GAIN_T * push_y
                if f == 1:
                    a = a + GAIN_S * push_x
                    b = b + GAIN_S * push_y
                base = (mix * cc) * g[f]
                plus = base + a
                minus = base - a
                flat = mix * g[f]
                pe[fl] = plus
                mw[fl] = minus
                pn[fl, 8:24, :] = flat + b
                mn[fl, 8:24, :] = flat - b
                packed = pack(packed, jnp.where(low_lane, plus, minus), fl)
                to_u = to_u + g[f] * (hm * ew[k, fl])
                to_v = to_v - g[f] * (0.5 * ns[k, fl])
            for f in range(4):
                fl = f * LEV + l
                own = -2.0 * (MIX[f] * cc + MIX[f]) * g[f]
                if f == 2:
                    own = own - to_u
                if f == 3:
                    own = own + to_v
                acc[fl] = own
            return packed, sum_u, sum_v

        packed, _, _ = levels(body, (blank, blank, blank))
        col_s[6 + n] = packed
        stage_rows(6 + n, mn, pn)
        launch(6 + n)

    def take(n, source):
        stage = (5 - n) % 3
        e = 6 + n
        arrive(e)
        put_rows(mn, 7, PAD, row_r[e, 0])
        put_rows(pn, 24, PAD, row_r[e, 1])
        received = halo(e)

        def body(l, carry):
            for f in range(4):
                fl = f * LEV + l
                w_side, e_side = sides(turn(received, fl), mw[fl], pe[fl])
                got = acc[fl] + w_side + e_side + pn[fl, 9:25, :] + mn[fl, 7:23, :]
                if stage == 2:
                    t2[fl] = (2.0 / 3.0) * source[fl] + got
                elif stage == 1:
                    t1[fl] = 0.25 * t2[fl] + got
                else:
                    new = (1.0 / 3.0) * source[fl] + 0.75 * t2[fl] + t1[fl] + got + dx[fl]
                    if n == 5:
                        grad[fl] = jnp.where(depth > l, new, 0.0)
                    else:
                        lam[fl] = new
            return carry

        levels(body, 0)

    prepare()
    layer_one(0)
    forward(0, None)
    fan_arrive(0)
    f1[...] = slot_sum(0, f0[...], fr1)
    fan_start(1)
    layer_two(0)
    forward(1, None)
    layer_three(0)
    fan_arrive(1)
    totals = slot_sum(1, f1[...], fr2)
    flux_sum = jnp.sum(totals[0:1, :], axis=1, keepdims=True)
    count_sum = jnp.sum(totals[1:2, :], axis=1, keepdims=True)
    mean = jnp.broadcast_to(flux_sum / count_sum, (ROWS, COLS))
    forcing = -FRESHWATER * (flux[...] - mean)
    forward(2, forcing)
    layer_one(1)
    forward(3, None)
    layer_two(1)
    forward(4, None)
    layer_three(1)
    forward(5, forcing)

    give(0, cot)
    back_out(1, cot)
    take(0, cot)
    give(1, t2)
    back_mid(1)
    back_in(1)
    take(1, cot)
    give(2, t1)
    weight_grads(1, False)
    take(2, cot)
    give(3, lam)
    back_out(0, lam)
    back_mid(0)
    take(3, lam)
    give(4, t2)
    weight_grads(0, True)
    fan_start(2)
    back_in(0)
    take(4, lam)
    give(5, t1)
    fan_arrive(2)
    c1[...] = slot_sum(2, gb[part(spot)], rs1)
    fan_start(3)
    take(5, lam)
    fan_arrive(3)
    scale = 1.0 / math.sqrt(lat_count * ROWS * lon_count * COLS)
    c2[...] = slot_sum(3, c1[...], rs2) * scale
    ag[part(spot)] = c2[...]
    fan_start(4)
    for e in range(12):
        drain(e)
    for stage in range(4):
        fan_drain(stage)
    fan_arrive(4)
    fan_drain(4)


def unpack(fin, grad, ag, o_fin, o_grad, g_win, g_bin, g_wmid, g_bmid, g_wout, g_bout):
    o_fin[...] = fin[...]
    o_grad[...] = grad[...]
    g_wmid[...] = ag[0:64, 0:HID]
    g_wout[...] = pltpu.roll(ag[0:COLS], 64, 1).T[0:FEAT, 0:HID]
    g_win[...] = ag[64:104, 0:HID]
    sums = ag[104:112]
    g_bin[...] = sums[0:1, 0:HID]
    g_bmid[...] = sums[1:2, 0:HID]
    g_bout[...] = sums[2:3, 0:FEAT]


def on_device(lat_count, lon_count, state, mask, flux, win, b_in, wmid, b_mid, wout, b_out, cot):
    def v(*shape):
        return pltpu.VMEM(shape, F32)

    near, far = lon_count // 2, lat_count * 2
    share = 128 // near
    vmem = pl.BlockSpec(memory_space=pltpu.VMEM)
    field = (FEAT, ROWS, COLS)
    tall = (FEAT, PAD, COLS)
    wide = (64, CELLS)
    out = pl.pallas_call(
        functools.partial(kernel, lat_count, lon_count),
        out_shape=[jax.ShapeDtypeStruct(shape, F32) for shape in (field, field, (128, COLS))],
        in_specs=[vmem] * 10,
        out_specs=[vmem] * 3,
        scratch_shapes=[
            v(6, *tall),
            v(6, *field),
            v(6, *field),
            v(*field),
            v(*field),
            v(*tall),
            v(*tall),
            v(*field),
            v(*field),
            v(*field),
            v(*field),
            v(2, *wide),
            v(2, *wide),
            v(2, *wide),
            v(*wide),
            v(*wide),
            v(*wide),
            v(*field),
            v(*field),
            v(*field),
            pltpu.VMEM((6, 64, 192), BF16),
            v(3, 64, COLS),
            v(COLS, COLS),
            v(128, COLS),
            v(near, share, COLS),
            v(share, COLS),
            v(far, share, COLS),
            v(share, COLS),
            v(8, COLS),
            v(near, 8, COLS),
            v(8, COLS),
            v(far, 8, COLS),
            v(12, 2, FEAT, COLS),
            v(12, 2, FEAT, COLS),
            v(12, ROWS, COLS),
            v(12, 2, ROWS, COLS),
            pltpu.SemaphoreType.DMA((12, 4)),
            pltpu.SemaphoreType.DMA((12, 4)),
            pltpu.SemaphoreType.DMA((5, max(near, far))),
            pltpu.SemaphoreType.DMA((5, max(near, far))),
        ],
        compiler_params=pltpu.CompilerParams(
            collective_id=0, has_side_effects=True, vmem_limit_bytes=60 * 1024 * 1024
        ),
    )(
        state.reshape(field),
        mask,
        flux,
        win,
        b_in.reshape(1, HID),
        wmid,
        b_mid.reshape(1, HID),
        wout.T,
        b_out.reshape(1, FEAT),
        cot.reshape(field),
    )
    out = pl.pallas_call(
        unpack,
        out_shape=[
            jax.ShapeDtypeStruct(shape, F32)
            for shape in (
                field,
                field,
                (FEAT, HID),
                (1, HID),
                (HID, HID),
                (1, HID),
                (FEAT, HID),
                (1, FEAT),
            )
        ],
        in_specs=[vmem] * 3,
        out_specs=[vmem] * 8,
    )(*out)
    shape4 = (4, LEV, ROWS, COLS)
    return (
        out[0].reshape(shape4),
        out[1].reshape(shape4),
        out[2],
        out[3].reshape(HID),
        out[4],
        out[5].reshape(HID),
        out[6].T,
        out[7].reshape(FEAT),
    )


def solution(mesh):
    block = P(None, None, "lat", "lon")
    return jax.shard_map(
        functools.partial(on_device, mesh.shape["lat"], mesh.shape["lon"]),
        mesh=mesh,
        in_specs=(
            block,
            P(None, "lat", "lon"),
            P("lat", "lon"),
            P(),
            P(),
            P(),
            P(),
            P(),
            P(),
            block,
        ),
        out_specs=(block, block, P(), P(), P(), P(), P(), P()),
        check_vma=False,
    )
```

```python
import functools
import math

import jax
import jax.numpy as jnp
from jax import lax
from jax.experimental import pallas as pl
from jax.experimental.pallas import tpu as pltpu
from jax.sharding import PartitionSpec as P

F32 = jnp.float32
BF16 = jnp.bfloat16
MESH = pl.DeviceIdType.MESH

LEV = 10
FEAT = 40
HID = 64
ROWS = 16
COLS = 128
CELLS = ROWS * COLS
TALL = 24
PAD = 32

LAT_LIMIT = 1.2
DT = 0.25
MIX = (0.1, 0.1, 0.15, 0.15)
GAIN_S = 0.5 * 0.8
GAIN_T = -0.5 * 0.2
FRESHWATER = 2.0
CHUNK = 512


def split(x):
    hi = x.astype(BF16)
    lo = (x - hi.astype(F32)).astype(BF16)
    return hi, lo


def kernel(
    lat_count,
    lon_count,
    state,
    mask,
    flux,
    win,
    b_in,
    wmid,
    b_mid,
    wout,
    b_out,
    cot,
    fin,
    grad,
    ag,
    xs,
    ewsum,
    ew,
    ns,
    pe,
    mw,
    pn,
    mn,
    acc,
    lam,
    t2,
    t1,
    zc,
    h1,
    h2,
    dout,
    da2,
    da1,
    mx,
    dx,
    dox,
    lhs,
    bcol,
    square,
    gb,
    rs1,
    c1,
    rs2,
    c2,
    f0,
    fr1,
    f1,
    fr2,
    row_s,
    row_r,
    col_s,
    col_r,
    xh,
    st,
    sd,
    dh,
    wrow_s,
    wrow_r,
    wst_s,
    wst_r,
    wc_s,
    wc_r,
    h_send,
    h_recv,
    w_send,
    w_recv,
    a_send,
    a_recv,
):
    lon = lax.axis_index("lon")
    lat = lax.axis_index("lat")
    east = lax.rem(lon + 1, lon_count)
    west = lax.rem(lon + lon_count - 1, lon_count)
    has_n = lat < lat_count - 1
    has_s = lat > 0
    halves = 2
    near = lon_count // halves
    far = lat_count * halves
    share = 128 // near
    half = lax.div(lon, jnp.int32(near))
    spot = lon - half * near

    def wrap(at, count):
        return at - count * lax.div(at, jnp.int32(count))

    near_spots = [wrap(spot + d, near) for d in range(near)]
    far_lats = [wrap(lat + d, lat_count) for d in range(lat_count)]
    far_lons = [half * near + spot, (1 - half) * near + spot]

    def along(d):
        return {"lon": half * near + near_spots[d], "lat": lat}

    def across(d):
        return {"lon": far_lons[d % halves], "lat": far_lats[d // halves]}

    north_id = {"lon": lon, "lat": lat + 1}
    south_id = {"lon": lon, "lat": lat - 1}
    east_id = {"lon": east, "lat": lat}
    west_id = {"lon": west, "lat": lat}
    ne_id = {"lon": east, "lat": lat + 1}
    nw_id = {"lon": west, "lat": lat + 1}
    se_id = {"lon": east, "lat": lat - 1}
    sw_id = {"lon": west, "lat": lat - 1}

    barrier = pltpu.get_barrier_semaphore()

    def greet(to):
        pl.semaphore_signal(barrier, inc=1, device_id=to, device_id_type=MESH)

    greet(east_id)
    greet(west_id)

    @pl.when(has_n)
    def _():
        greet(north_id)
        greet(ne_id)
        greet(nw_id)

    @pl.when(has_s)
    def _():
        greet(south_id)
        greet(se_id)
        greet(sw_id)

    for d in range(1, near):
        greet(along(d))
    for d in range(1, far):
        greet(across(d))

    lane24 = lax.broadcasted_iota(jnp.int32, (TALL, COLS), 1)
    row24 = lax.broadcasted_iota(jnp.int32, (TALL, COLS), 0)
    lane = lane24[0:ROWS]
    row = row24[0:ROWS]
    odd_lane = lax.rem(lane, 2) == 1
    low_lane = lane < 64
    place = row24 + jnp.where(row24 < 16, 0, jnp.where(row24 < 20, -19, -5))
    grow = jnp.clip(place + lat * ROWS, 0, lat_count * ROWS - 1).astype(F32)
    phi = LAT_LIMIT * (2.0 * (grow + 0.5) / (lat_count * ROWS) - 1.0)
    sq = phi * phi
    cosine = jnp.ones_like(phi)
    sine = jnp.ones_like(phi)
    for n in range(8, 0, -1):
        cosine = 1.0 - cosine * sq * (1.0 / ((2 * n - 1) * (2 * n)))
        sine = 1.0 - sine * sq * (1.0 / ((2 * n) * (2 * n + 1)))
    inv24 = 1.0 / cosine
    cor24 = sine * phi
    hm24 = 0.5 * inv24
    cc24 = inv24 * inv24
    cor, hm, cc = cor24[0:ROWS], hm24[0:ROWS], cc24[0:ROWS]
    depth = mask[0]
    for l in range(1, LEV):
        depth = depth + mask[l]
    depth_own = depth.astype(F32)
    group = lax.div(lane24, jnp.int32(12))
    slot = lane24 - 12 * group

    def hcopy(e, d):
        if d == 0:
            src, dst, to = row_s.at[e, 0], row_r.at[e, 0], north_id
        elif d == 1:
            src, dst, to = row_s.at[e, 1], row_r.at[e, 1], south_id
        elif d == 2:
            src, dst, to = col_s.at[e], col_r.at[e, 0], east_id
        else:
            src, dst, to = col_s.at[e], col_r.at[e, 1], west_id
        return pltpu.make_async_remote_copy(
            src_ref=src,
            dst_ref=dst,
            send_sem=h_send.at[e, d],
            recv_sem=h_recv.at[e, d],
            device_id=to,
            device_id_type=MESH,
        )

    def launch(e):
        @pl.when(has_n)
        def _():
            hcopy(e, 0).start()

        @pl.when(has_s)
        def _():
            hcopy(e, 1).start()

        hcopy(e, 2).start()
        hcopy(e, 3).start()

    def arrive(e):
        @pl.when(has_s)
        def _():
            hcopy(e, 0).wait_recv()

        @pl.when(has_n)
        def _():
            hcopy(e, 1).wait_recv()

        hcopy(e, 2).wait_recv()
        hcopy(e, 3).wait_recv()

    def drain(e):
        @pl.when(has_n)
        def _():
            hcopy(e, 0).wait_send()

        @pl.when(has_s)
        def _():
            hcopy(e, 1).wait_send()

        hcopy(e, 2).wait_send()
        hcopy(e, 3).wait_send()

    def wcopy(e, d):
        count = 48 if e == 0 else FEAT
        fields = 5 if e == 0 else 4
        if d < 2:
            src = wrow_s.at[e, d, :, 0:count]
            dst = wrow_r.at[e, d, :, 0:count]
            to = (north_id, south_id)[d]
        elif d < 4:
            src = wst_s.at[e, 0:fields]
            dst = wst_r.at[e, d - 2, 0:fields]
            to = (east_id, west_id)[d - 2]
        else:
            src = wc_s.at[e, (d - 4) // 3]
            dst = wc_r.at[e, d - 4]
            to = (north_id, ne_id, nw_id, south_id, se_id, sw_id)[d - 4]
        return pltpu.make_async_remote_copy(
            src_ref=src,
            dst_ref=dst,
            send_sem=w_send.at[e, d],
            recv_sem=w_recv.at[e, d],
            device_id=to,
            device_id_type=MESH,
        )

    north_ones = (0, 4, 5, 6)
    south_ones = (1, 7, 8, 9)

    def wide_launch(e):
        @pl.when(has_n)
        def _():
            for d in north_ones:
                wcopy(e, d).start()

        @pl.when(has_s)
        def _():
            for d in south_ones:
                wcopy(e, d).start()

        wcopy(e, 2).start()
        wcopy(e, 3).start()

    def wide_arrive(e):
        @pl.when(has_s)
        def _():
            for d in north_ones:
                wcopy(e, d).wait_recv()

        @pl.when(has_n)
        def _():
            for d in south_ones:
                wcopy(e, d).wait_recv()

        wcopy(e, 2).wait_recv()
        wcopy(e, 3).wait_recv()

    def wide_drain(e):
        @pl.when(has_n)
        def _():
            for d in north_ones:
                wcopy(e, d).wait_send()

        @pl.when(has_s)
        def _():
            for d in south_ones:
                wcopy(e, d).wait_send()

        wcopy(e, 2).wait_send()
        wcopy(e, 3).wait_send()

    def strip_pack(strip, value, l):
        low = pltpu.roll(value, 12 * l + 3, 1)
        high = pltpu.roll(value, (12 * l + 9) % COLS, 1)
        here = (lane >= 12 * l + 3) & (lane < 12 * l + 6)
        there = (lane >= 12 * l + 6) & (lane < 12 * l + 9)
        return jnp.where(here, low, jnp.where(there, high, strip))

    def wide_stage(e, strips):
        k = 3 * e
        for j in range(3):
            wrow_s[e, 0, j, 0:FEAT] = take_rows(xs.at[k], 21 + j, PAD)
            wrow_s[e, 1, j, 0:FEAT] = take_rows(xs.at[k], 8 + j, PAD)
            if e == 0:
                wrow_s[e, 0, j, 40:48] = jnp.broadcast_to(depth_own[13 + j : 14 + j], (8, COLS))
                wrow_s[e, 1, j, 40:48] = jnp.broadcast_to(depth_own[j : j + 1], (8, COLS))
        if e == 1:
            wc_s[e] = jnp.zeros((2, 16, COLS), F32)
        for f, strip in enumerate(strips):
            wst_s[e, f] = strip
            wc_s[e, 0, 3 * f : 3 * f + 3] = strip[13:16]
            wc_s[e, 1, 3 * f : 3 * f + 3] = strip[0:3]

    def pick(from_west, own, from_east, slots):
        return jnp.where(
            slots < 3,
            pltpu.roll(from_west, COLS - 6, 1),
            jnp.where(slots >= 9, pltpu.roll(from_east, 6, 1), own),
        )

    def wide_unpack(e):
        k = 3 * e
        put_rows(xs.at[k], 7, PAD, wrow_r[e, 0, 2, 0:FEAT])
        put_rows(xs.at[k], 24, PAD, wrow_r[e, 1, 0, 0:FEAT])
        for j in range(3):
            put_rows(xh.at[k], j, 8, wrow_r[e, 0, j, 0:FEAT])
            put_rows(xh.at[k], 5 + j, 8, wrow_r[e, 1, j, 0:FEAT])
        put_rows(xh.at[k], 3, 8, take_rows(xs.at[k], 8, PAD))
        put_rows(xh.at[k], 4, 8, take_rows(xs.at[k], 23, PAD))
        slots = slot[0:ROWS]
        below = pick(wc_r[e, 1], wc_r[e, 0], wc_r[e, 2], slots)
        above = pick(wc_r[e, 4], wc_r[e, 3], wc_r[e, 5], slots)
        for f in range(5 if e == 0 else 4):
            own = pick(wst_r[e, 0, f], wst_s[e, f], wst_r[e, 1, f], slots)
            to = st.at[k, f] if f < 4 else sd
            to[0:16, :] = own
            to[16:19, :] = below[3 * f : 3 * f + 3]
            to[19:20, :] = own[0:1]
            to[20:21, :] = own[15:16]
            to[21:24, :] = above[3 * f : 3 * f + 3]
        if e == 0:
            dh[...] = jnp.zeros((8, COLS), F32)
            for j in range(3):
                dh[j : j + 1] = wrow_r[e, 0, j, 40:41]
                dh[5 + j : 6 + j] = wrow_r[e, 1, j, 40:41]

    def take_rows(ref, r, count):
        return ref.reshape(FEAT * count, COLS)[pl.ds(r, FEAT, stride=count), :]

    def put_rows(ref, r, count, value):
        ref.reshape(FEAT * count, COLS)[pl.ds(r, FEAT, stride=count), :] = value

    def pack(packed, value, fl):
        turned = pltpu.roll(value, 2 * fl + 1, 1)
        return jnp.where(lane // 2 == fl, turned, packed)

    def part(at):
        return pl.ds(pl.multiple_of(at * share, share), share)

    def others(stage):
        return range(1, far if stage in (1, 3) else near)

    def fan(stage, d, src, dst, to):
        return pltpu.make_async_remote_copy(
            src_ref=src,
            dst_ref=dst,
            send_sem=a_send.at[stage, d],
            recv_sem=a_recv.at[stage, d],
            device_id=to,
            device_id_type=MESH,
        )

    def fan_copy(stage, d):
        if stage == 0:
            return fan(stage, d, f0, fr1.at[d], along(d))
        if stage == 1:
            return fan(stage, d, f1, fr2.at[d], across(d))
        if stage == 2:
            return fan(stage, d, gb.at[part(near_spots[d])], rs1.at[d], along(d))
        if stage == 3:
            return fan(stage, d, c1, rs2.at[d], across(d))
        return fan(stage, d, c2, ag.at[part(spot)], along(d))

    def fan_start(stage):
        for d in others(stage):
            fan_copy(stage, d).start()

    def fan_arrive(stage):
        for d in others(stage):
            fan_copy(stage, d).wait_recv()

    def fan_drain(stage):
        for d in others(stage):
            fan_copy(stage, d).wait_send()

    def slot_sum(stage, own, slots):
        total = own
        for d in others(stage):
            total = total + slots[d]
        return total

    def levels(body, carry):
        for l in range(LEV):
            carry = body(l, carry)
        return carry

    blank = jnp.zeros((ROWS, COLS), F32)
    strips = [blank] * 5
    for l in range(LEV):
        wet = depth > l
        for f in range(4):
            fl = f * LEV + l
            x = jnp.where(wet, state[fl], 0.0)
            xs[0, fl, 8:24, :] = x
            strips[f] = strip_pack(strips[f], x, l)
        strips[4] = strip_pack(strips[4], depth_own, l)
    wc_s[0] = jnp.zeros((2, 16, COLS), F32)
    wide_stage(0, strips)

    def stage_rows(e, north_ref, south_ref):
        row_s[e, 0] = take_rows(north_ref, 23, PAD)
        row_s[e, 1] = take_rows(south_ref, 8, PAD)

    wet_top = depth > 0
    part_flux = jnp.sum(jnp.where(wet_top, flux[...], 0.0), axis=0, keepdims=True)
    part_count = jnp.sum(jnp.where(wet_top, 1.0, 0.0), axis=0, keepdims=True)
    row8 = lax.broadcasted_iota(jnp.int32, (8, COLS), 0)
    f0[...] = jnp.where(
        row8 == 0,
        jnp.broadcast_to(part_flux, (8, COLS)),
        jnp.where(row8 == 1, jnp.broadcast_to(part_count, (8, COLS)), 0.0),
    )

    meet = near + far + 3 * has_n.astype(jnp.int32) + 3 * has_s.astype(jnp.int32)
    pl.semaphore_wait(barrier, meet)
    wide_launch(0)
    fan_start(0)

    @pl.when(jnp.logical_not(has_s))
    def _():
        for e in range(6):
            row_r[e, 0] = jnp.zeros((FEAT, COLS), F32)
        for e in range(2):
            wrow_r[e, 0] = jnp.zeros((3, 48, COLS), F32)
            for d in range(3):
                wc_r[e, d] = jnp.zeros((16, COLS), F32)

    @pl.when(jnp.logical_not(has_n))
    def _():
        for e in range(6):
            row_r[e, 1] = jnp.zeros((FEAT, COLS), F32)
        for e in range(2):
            wrow_r[e, 1] = jnp.zeros((3, 48, COLS), F32)
            for d in range(3, 6):
                wc_r[e, d] = jnp.zeros((16, COLS), F32)

    def weight(at, value):
        hi, lo = split(value)
        lhs[at, :, 0:64] = hi
        lhs[at, :, 64:128] = hi
        lhs[at, :, 128:192] = lo

    def both(value_ref, rows, cols, plain, turned):
        square[...] = jnp.zeros((COLS, COLS), F32)
        square[0:rows, 0:cols] = value_ref[...]
        whole = square[...]
        weight(plain, whole[0:64, 0:64])
        weight(turned, whole.T[0:64, 0:64])

    def prepare():
        both(wout, FEAT, HID, 2, 3)
        both(wmid, HID, HID, 4, 1)
        both(win, FEAT, HID, 5, 0)
        square[...] = jnp.zeros((COLS, COLS), F32)
        square[0:1, 0:HID] = b_in[...]
        square[1:2, 0:HID] = b_mid[...]
        square[2:3, 0:FEAT] = b_out[...]
        turned = square[...].T
        for at in range(3):
            bcol[at] = jnp.broadcast_to(turned[0:64, at : at + 1], (64, COLS))
        for s in range(2):
            zc[s, FEAT:64, :] = jnp.zeros((64 - FEAT, CELLS), F32)
        dout[FEAT:64, :] = jnp.zeros((64 - FEAT, CELLS), F32)
        gb[112:128] = jnp.zeros((16, COLS), F32)
        put_rows(mn, 7, PAD, jnp.zeros((FEAT, COLS), F32))
        put_rows(pn, 24, PAD, jnp.zeros((FEAT, COLS), F32))

    def product(at, x):
        hi, lo = split(x)
        return jnp.dot(
            lhs[at], jnp.concatenate([hi, lo, hi], axis=0), preferred_element_type=F32
        )

    def bias(at):
        return jnp.concatenate([bcol[at]] * (CHUNK // COLS), axis=1)

    def gather(ref, first, count, out):
        for r in range(ROWS):
            out[0:FEAT, r * COLS : (r + 1) * COLS] = take_rows(ref, first + r, count)

    chunks = [pl.ds(c * CHUNK, CHUNK) for c in range(CELLS // CHUNK)]

    def layer_one(s):
        gather(xs.at[3 * s], 8, PAD, zc.at[s])
        for c in chunks:
            h1[s, :, c] = jnp.tanh(product(0, zc[s, :, c]) + bias(0))

    def layer_two(s):
        for c in chunks:
            h2[s, :, c] = jnp.tanh(product(1, h1[s, :, c]) + bias(1))

    def scatter(ref, n, value):
        for j in range(CHUNK // COLS):
            put_rows(
                ref, n * (CHUNK // COLS) + j, ROWS, value[0:FEAT, j * COLS : (j + 1) * COLS]
            )

    def layer_three(s):
        for n, c in enumerate(chunks):
            scatter(mx, n, product(2, h2[s, :, c]) + bias(2))

    def back_out(s, source):
        def body(l, carry):
            wet = depth > l
            for f in range(4):
                fl = f * LEV + l
                dox[fl] = jnp.where(wet, DT * source[fl], 0.0)
            return carry

        levels(body, 0)
        gather(dox, 0, ROWS, dout)
        for c in chunks:
            h = h2[s, :, c]
            da2[:, c] = product(3, dout[:, c]) * (1.0 - h * h)

    def back_mid(s):
        for c in chunks:
            h = h1[s, :, c]
            da1[:, c] = product(4, da2[:, c]) * (1.0 - h * h)

    def back_in(s):
        for n, c in enumerate(chunks):
            scatter(dx, n, product(5, da1[:, c]))

    def outer(left_ref, right_ref):
        total = jnp.zeros((144, COLS), F32)
        ones = jnp.ones((16, CHUNK), BF16)
        for c in chunks:
            hi, lo = split(left_ref[:, c])
            r_hi, r_lo = split(right_ref[:, c])
            total = total + lax.dot_general(
                jnp.concatenate([hi, lo, ones], axis=0),
                jnp.concatenate([r_hi, r_lo], axis=0),
                (((1,), (1,)), ((), ())),
                preferred_element_type=F32,
            )
        folded = total + pltpu.roll(total, 64, 1)
        return folded[0:64] + total[64:128], folded[128:136]

    def weight_grads(s, add):
        g_in, s_in = outer(zc.at[s], da1)
        g_mid, s_mid = outer(h1.at[s], da2)
        g_out, s_out = outer(h2.at[s], dout)
        wide = lax.broadcasted_iota(jnp.int32, (64, COLS), 1) < 64
        low8 = lax.broadcasted_iota(jnp.int32, (8, COLS), 1) < 64
        top = jnp.where(wide, g_mid, pltpu.roll(g_out, 64, 1))
        low = jnp.where(wide, g_in, 0.0)[0:FEAT]
        sums = jnp.where(
            row8 == 0, s_in, jnp.where(row8 == 1, s_mid, jnp.where(row8 == 2, s_out, 0.0))
        )
        sums = jnp.where(low8, sums, 0.0)
        if add:
            gb[0:64] = gb[0:64] + top
            gb[64:104] = gb[64:104] + low
            gb[104:112] = gb[104:112] + sums
        else:
            gb[0:64] = top
            gb[64:104] = low
            gb[104:112] = sums

    first_lane = lane == 0
    last_lane = lane == COLS - 1

    def add_rows(ref, r, value):
        view = ref.reshape(FEAT * ROWS, COLS)
        view[pl.ds(r, FEAT, stride=ROWS), :] = view[pl.ds(r, FEAT, stride=ROWS), :] + value

    def tendency(f, q, d_x, d_y, sum_x, sum_y, u, v, p_x, p_y, coef):
        c_hm, c_cc, c_cor = coef
        mix = MIX[f]
        change = (
            (mix * c_cc) * (sum_x - 2.0 * q)
            + mix * (sum_y - 2.0 * q)
            - ((u * c_hm) * d_x + (v * 0.5) * d_y)
        )
        if f == 2:
            change = change + (c_cor * v - p_x * c_hm)
        if f == 3:
            change = change - (c_cor * u + p_y * 0.5)
        return DT * change

    def rise(own, edge):
        own_n = jnp.where(
            row == 15, jnp.broadcast_to(edge[5:6], (ROWS, COLS)), pltpu.roll(own, 15, 0)
        )
        own_s = jnp.where(
            row == 0, jnp.broadcast_to(edge[2:3], (ROWS, COLS)), pltpu.roll(own, 1, 0)
        )
        return (
            jnp.concatenate([own_n, pltpu.roll(edge, 7, 0)], axis=0),
            jnp.concatenate([own_s, pltpu.roll(edge, 1, 0)], axis=0),
        )

    def mend(edge, own):
        rows8 = row24[0:8]
        first = jnp.broadcast_to(own[0:1], (8, COLS))
        last = jnp.broadcast_to(own[15:16], (8, COLS))
        return jnp.where(rows8 == 3, first, jnp.where(rows8 == 4, last, edge))

    def strip_section(k):
        start, stage = 3 * (k // 3), k % 3
        wet = (group.astype(F32) < sd[...]) & (lane24 < 12 * LEV)
        q = [st[k, f] for f in range(4)]
        d_x, d_y, sum_x, sum_y = [], [], [], []
        for f in range(4):
            east_q = pltpu.roll(q[f], COLS - 1, 1)
            west_q = pltpu.roll(q[f], 1, 1)
            north_q, south_q = rise(q[f][0:16], q[f][16:24])
            d_x.append(east_q - west_q)
            d_y.append(north_q - south_q)
            sum_x.append(east_q + west_q)
            sum_y.append(north_q + south_q)

        def down(slope):
            total = GAIN_T * slope[0] + GAIN_S * slope[1]
            for hop in (12, 24, 48, 96):
                total = total + jnp.where(lane24 >= hop, pltpu.roll(total, hop, 1), 0.0)
            return total

        p_x, p_y = down(d_x), down(d_y)
        for f in range(4):
            change = tendency(
                f, q[f], d_x[f], d_y[f], sum_x[f], sum_y[f], q[2], q[3], p_x, p_y,
                (hm24, cc24, cor24),
            )
            moved = q[f] + jnp.where(wet, change, 0.0)
            new = moved if stage == 0 else 0.75 * st[start, f] + 0.25 * moved
            st[k + 1, f, 0:16, :] = new[0:16]
            st[k + 1, f, 16:24, :] = mend(new[16:24], new[0:16])

    def forward(k, forcing):
        e, start, stage = k // 3, 3 * (k // 3), k % 3
        if stage == 0:
            wide_arrive(e)
            wide_unpack(e)
        tall = TALL if stage < 2 else ROWS
        lanes = lane24[0:tall]
        first, last = lanes == 0, lanes == COLS - 1
        coef = (hm24[0:tall], cc24[0:tall], cor24[0:tall])
        if tall == TALL:
            deep = jnp.concatenate([depth_own, dh[...]], axis=0)
        else:
            deep = depth_own
        rows8 = row24[0:8]
        strips = [blank] * 4
        edges = [st[k, f, 0:tall, :] for f in range(4)]
        press_x = press_y = jnp.zeros((tall, COLS), F32)

        def value(at, fl):
            own = xs[at, fl, 8:24, :]
            return jnp.concatenate([own, xh[at, fl]], axis=0) if tall == TALL else own

        for l in range(LEV):
            for f in range(4):
                fl = f * LEV + l
                q = value(k, fl)
                from_w = pltpu.roll(edges[f], (2 * COLS - 2 - 12 * l) % COLS, 1)
                from_e = pltpu.roll(edges[f], (2 * COLS - 10 - 12 * l) % COLS, 1)
                w_side = jnp.where(first, from_w, pltpu.roll(q, 1, 1))
                e_side = jnp.where(last, from_e, pltpu.roll(q, COLS - 1, 1))
                ew[k, fl, 0:tall] = e_side - w_side
                ewsum[fl, 0:tall] = e_side + w_side

        for l in range(LEV):
            wet = deep > float(l)
            u = value(k, 2 * LEV + l)
            v = value(k, 3 * LEV + l)
            for f in range(4):
                fl = f * LEV + l
                q = value(k, fl)
                north = xs[k, fl, 9:25, :]
                south = xs[k, fl, 7:23, :]
                if tall == TALL:
                    edge = xh[k, fl]
                    north = jnp.concatenate([north, pltpu.roll(edge, 7, 0)], axis=0)
                    south = jnp.concatenate([south, pltpu.roll(edge, 1, 0)], axis=0)
                d_x = ew[k, fl, 0:tall]
                d_y = north - south
                ns[k, fl] = d_y[0:ROWS]
                if f < 2:
                    press_x = press_x + (GAIN_T, GAIN_S)[f] * d_x
                    press_y = press_y + (GAIN_T, GAIN_S)[f] * d_y
                change = tendency(
                    f, q, d_x, d_y, ewsum[fl, 0:tall], north + south, u, v, press_x, press_y, coef
                )
                moved = q + jnp.where(wet, change, 0.0)
                if stage == 0:
                    new = moved
                elif stage == 1:
                    new = 0.75 * value(start, fl) + 0.25 * moved
                else:
                    given = mx[fl]
                    if f == 1 and l == 0:
                        given = given + forcing
                    new = (
                        (1.0 / 3.0) * value(start, fl)
                        + (2.0 / 3.0) * moved
                        + jnp.where(wet, DT * given, 0.0)
                    )
                if stage < 2:
                    own, edge = new[0:ROWS], new[ROWS:TALL]
                    xs[k + 1, fl, 8:24, :] = own
                    xs[k + 1, fl, 7:8, :] = edge[2:3]
                    xs[k + 1, fl, 24:25, :] = edge[5:6]
                    xh[k + 1, fl] = mend(edge, own)
                elif k == 2:
                    xs[k + 1, fl, 8:24, :] = new
                    strips[f] = strip_pack(strips[f], new, l)
                else:
                    fin[fl] = new
        if stage < 2:
            strip_section(k)
        elif k == 2:
            wide_stage(1, strips)
            wide_launch(1)

    def give(n, source):
        k, stage = 5 - n, (5 - n) % 3
        scale = (1.0, 0.25, 2.0 / 3.0)[stage]

        def body(t, carry):
            packed, sum_u, sum_v = carry
            l = LEV - 1 - t
            wet = depth > l
            g = [jnp.where(wet, (DT * scale) * source[f * LEV + l], 0.0) for f in range(4)]
            sum_u = sum_u + g[2]
            sum_v = sum_v + g[3]
            u = xs[k, 2 * LEV + l, 8:24, :]
            v = xs[k, 3 * LEV + l, 8:24, :]
            uh = u * hm
            vh = v * 0.5
            push_x = hm * sum_u
            push_y = 0.5 * sum_v
            for f in range(4):
                fl = f * LEV + l
                mix = MIX[f]
                a = uh * g[f]
                b = vh * g[f]
                if f == 0:
                    a = a + GAIN_T * push_x
                    b = b + GAIN_T * push_y
                if f == 1:
                    a = a + GAIN_S * push_x
                    b = b + GAIN_S * push_y
                base = (mix * cc) * g[f]
                plus = base + a
                minus = base - a
                flat = mix * g[f]
                pe[fl] = plus
                mw[fl] = minus
                pn[fl, 8:24, :] = flat + b
                mn[fl, 8:24, :] = flat - b
                packed = pack(packed, jnp.where(low_lane, plus, minus), fl)
            return packed, sum_u, sum_v

        packed, _, _ = levels(body, (blank, blank, blank))
        col_s[n] = packed
        stage_rows(n, mn, pn)
        launch(n)

    def keep(n, source):
        k, stage = 5 - n, (5 - n) % 3
        scale = (1.0, 0.25, 2.0 / 3.0)[stage]
        for l in range(LEV):
            wet = depth > l
            g = [jnp.where(wet, (DT * scale) * source[f * LEV + l], 0.0) for f in range(4)]
            along_x = along_y = blank
            for f in range(4):
                along_x = along_x + g[f] * ew[k, f * LEV + l, 0:ROWS]
                along_y = along_y + g[f] * ns[k, f * LEV + l]
            to_u = cor * g[3] + hm * along_x
            to_v = cor * g[2] - 0.5 * along_y
            for f in range(4):
                fl = f * LEV + l
                own = -2.0 * (MIX[f] * cc + MIX[f]) * g[f]
                if f == 2:
                    own = own - to_u
                if f == 3:
                    own = own + to_v
                w_side = jnp.where(first_lane, 0.0, pltpu.roll(mw[fl], 1, 1))
                e_side = jnp.where(last_lane, 0.0, pltpu.roll(pe[fl], COLS - 1, 1))
                acc[fl] = own + w_side + e_side + pn[fl, 9:25, :] + mn[fl, 7:23, :]

    def take(n, source):
        stage = (5 - n) % 3
        e = n
        arrive(e)
        add_rows(acc, 0, row_r[e, 0])
        add_rows(acc, 15, row_r[e, 1])
        received = jnp.where(
            odd_lane, pltpu.roll(col_r[e, 0], 1, 1), pltpu.roll(col_r[e, 1], COLS - 1, 1)
        )

        def body(l, carry):
            for f in range(4):
                fl = f * LEV + l
                turned = pltpu.roll(received, COLS - 1 - 2 * fl, 1)
                got = acc[fl] + jnp.where(first_lane | last_lane, turned, 0.0)
                if stage == 2:
                    t2[fl] = (2.0 / 3.0) * source[fl] + got
                elif stage == 1:
                    t1[fl] = 0.25 * t2[fl] + got
                else:
                    new = (1.0 / 3.0) * source[fl] + 0.75 * t2[fl] + t1[fl] + got + dx[fl]
                    if n == 5:
                        grad[fl] = jnp.where(depth > l, new, 0.0)
                    else:
                        lam[fl] = new
            return carry

        levels(body, 0)

    prepare()
    layer_one(0)
    layer_two(0)
    layer_three(0)
    fan_arrive(0)
    f1[...] = slot_sum(0, f0[...], fr1)
    fan_start(1)
    forward(0, None)
    forward(1, None)
    fan_arrive(1)
    totals = slot_sum(1, f1[...], fr2)
    flux_sum = jnp.sum(totals[0:1, :], axis=1, keepdims=True)
    count_sum = jnp.sum(totals[1:2, :], axis=1, keepdims=True)
    mean = jnp.broadcast_to(flux_sum / count_sum, (ROWS, COLS))
    forcing = -FRESHWATER * (flux[...] - mean)
    forward(2, forcing)
    layer_one(1)
    layer_two(1)
    layer_three(1)
    back_out(1, cot)
    back_mid(1)
    back_in(1)
    forward(3, None)
    forward(4, None)

    give(0, cot)
    forward(5, forcing)
    keep(0, cot)
    take(0, cot)
    give(1, t2)
    keep(1, t2)
    weight_grads(1, False)
    take(1, cot)
    give(2, t1)
    keep(2, t1)
    take(2, cot)
    give(3, lam)
    keep(3, lam)
    back_out(0, lam)
    back_mid(0)
    take(3, lam)
    give(4, t2)
    keep(4, t2)
    weight_grads(0, True)
    fan_start(2)
    back_in(0)
    take(4, lam)
    give(5, t1)
    keep(5, t1)
    fan_arrive(2)
    c1[...] = slot_sum(2, gb[part(spot)], rs1)
    fan_start(3)
    take(5, lam)
    fan_arrive(3)
    scale = 1.0 / math.sqrt(lat_count * ROWS * lon_count * COLS)
    c2[...] = slot_sum(3, c1[...], rs2) * scale
    ag[part(spot)] = c2[...]
    fan_start(4)
    for e in range(6):
        drain(e)
    for e in range(2):
        wide_drain(e)
    for stage in range(4):
        fan_drain(stage)
    fan_arrive(4)
    fan_drain(4)


def unpack(fin, grad, ag, o_fin, o_grad, g_win, g_bin, g_wmid, g_bmid, g_wout, g_bout):
    o_fin[...] = fin[...]
    o_grad[...] = grad[...]
    g_wmid[...] = ag[0:64, 0:HID]
    g_wout[...] = pltpu.roll(ag[0:COLS], 64, 1).T[0:FEAT, 0:HID]
    g_win[...] = ag[64:104, 0:HID]
    sums = ag[104:112]
    g_bin[...] = sums[0:1, 0:HID]
    g_bmid[...] = sums[1:2, 0:HID]
    g_bout[...] = sums[2:3, 0:FEAT]


def on_device(lat_count, lon_count, state, mask, flux, win, b_in, wmid, b_mid, wout, b_out, cot):
    def v(*shape):
        return pltpu.VMEM(shape, F32)

    near, far = lon_count // 2, lat_count * 2
    share = 128 // near
    vmem = pl.BlockSpec(memory_space=pltpu.VMEM)
    field = (FEAT, ROWS, COLS)
    tall = (FEAT, PAD, COLS)
    wide = (64, CELLS)
    out = pl.pallas_call(
        functools.partial(kernel, lat_count, lon_count),
        out_shape=[jax.ShapeDtypeStruct(shape, F32) for shape in (field, field, (128, COLS))],
        in_specs=[vmem] * 10,
        out_specs=[vmem] * 3,
        scratch_shapes=[
            v(6, *tall),
            v(FEAT, TALL, COLS),
            v(6, FEAT, TALL, COLS),
            v(6, *field),
            v(*field),
            v(*field),
            v(*tall),
            v(*tall),
            v(*field),
            v(*field),
            v(*field),
            v(*field),
            v(2, *wide),
            v(2, *wide),
            v(2, *wide),
            v(*wide),
            v(*wide),
            v(*wide),
            v(*field),
            v(*field),
            v(*field),
            pltpu.VMEM((6, 64, 192), BF16),
            v(3, 64, COLS),
            v(COLS, COLS),
            v(128, COLS),
            v(near, share, COLS),
            v(share, COLS),
            v(far, share, COLS),
            v(share, COLS),
            v(8, COLS),
            v(near, 8, COLS),
            v(8, COLS),
            v(far, 8, COLS),
            v(6, 2, FEAT, COLS),
            v(6, 2, FEAT, COLS),
            v(6, ROWS, COLS),
            v(6, 2, ROWS, COLS),
            v(6, FEAT, 8, COLS),
            v(6, 4, TALL, COLS),
            v(TALL, COLS),
            v(8, COLS),
            v(2, 2, 3, 48, COLS),
            v(2, 2, 3, 48, COLS),
            v(2, 5, ROWS, COLS),
            v(2, 2, 5, ROWS, COLS),
            v(2, 2, 16, COLS),
            v(2, 6, 16, COLS),
            pltpu.SemaphoreType.DMA((6, 4)),
            pltpu.SemaphoreType.DMA((6, 4)),
            pltpu.SemaphoreType.DMA((2, 10)),
            pltpu.SemaphoreType.DMA((2, 10)),
            pltpu.SemaphoreType.DMA((5, max(near, far))),
            pltpu.SemaphoreType.DMA((5, max(near, far))),
        ],
        compiler_params=pltpu.CompilerParams(
            collective_id=0, has_side_effects=True, vmem_limit_bytes=60 * 1024 * 1024
        ),
    )(
        state.reshape(field),
        mask,
        flux,
        win,
        b_in.reshape(1, HID),
        wmid,
        b_mid.reshape(1, HID),
        wout.T,
        b_out.reshape(1, FEAT),
        cot.reshape(field),
    )
    out = pl.pallas_call(
        unpack,
        out_shape=[
            jax.ShapeDtypeStruct(shape, F32)
            for shape in (
                field,
                field,
                (FEAT, HID),
                (1, HID),
                (HID, HID),
                (1, HID),
                (FEAT, HID),
                (1, FEAT),
            )
        ],
        in_specs=[vmem] * 3,
        out_specs=[vmem] * 8,
    )(*out)
    shape4 = (4, LEV, ROWS, COLS)
    return (
        out[0].reshape(shape4),
        out[1].reshape(shape4),
        out[2],
        out[3].reshape(HID),
        out[4],
        out[5].reshape(HID),
        out[6].T,
        out[7].reshape(FEAT),
    )


def solution(mesh):
    block = P(None, None, "lat", "lon")
    return jax.shard_map(
        functools.partial(on_device, mesh.shape["lat"], mesh.shape["lon"]),
        mesh=mesh,
        in_specs=(
            block,
            P(None, "lat", "lon"),
            P("lat", "lon"),
            P(),
            P(),
            P(),
            P(),
            P(),
            P(),
            block,
        ),
        out_specs=(block, block, P(), P(), P(), P(), P(), P()),
        check_vma=False,
    )
```

```python
import functools
import math

import jax
import jax.numpy as jnp
from jax import lax
from jax.experimental import pallas as pl
from jax.experimental.pallas import tpu as pltpu
from jax.sharding import PartitionSpec as P

F32 = jnp.float32
BF16 = jnp.bfloat16
MESH = pl.DeviceIdType.MESH

LEV = 10
FEAT = 40
HID = 64
ROWS = 16
COLS = 128
CELLS = ROWS * COLS
TALL = 24
PAD = 32

LAT_LIMIT = 1.2
DT = 0.25
MIX = (0.1, 0.1, 0.15, 0.15)
GAIN_S = 0.5 * 0.8
GAIN_T = -0.5 * 0.2
FRESHWATER = 2.0
CHUNK = 512


def split(x):
    hi = x.astype(BF16)
    lo = (x - hi.astype(F32)).astype(BF16)
    return hi, lo


def kernel(
    lat_count,
    lon_count,
    state,
    mask,
    flux,
    win,
    b_in,
    wmid,
    b_mid,
    wout,
    b_out,
    cot,
    fin,
    grad,
    ag,
    xs,
    ewsum,
    ew,
    ns,
    pe,
    mw,
    pn,
    mn,
    acc,
    lam,
    t2,
    t1,
    zc,
    h1,
    h2,
    dout,
    da2,
    da1,
    mx,
    dx,
    dox,
    lhs,
    bcol,
    square,
    gb,
    rs1,
    c1,
    rs2,
    c2,
    f0,
    fr1,
    f1,
    fr2,
    row_s,
    row_r,
    col_s,
    col_r,
    xh,
    st,
    sd,
    dh,
    wrow_s,
    wrow_r,
    wst_s,
    wst_r,
    wc_s,
    wc_r,
    t2h,
    t1h,
    t2s,
    t1s,
    tp,
    tm,
    sdx,
    sdy,
    pe24,
    mw24,
    acc24,
    pnh,
    mnh,
    h_send,
    h_recv,
    w_send,
    w_recv,
    a_send,
    a_recv,
):
    lon = lax.axis_index("lon")
    lat = lax.axis_index("lat")
    east = lax.rem(lon + 1, lon_count)
    west = lax.rem(lon + lon_count - 1, lon_count)
    has_n = lat < lat_count - 1
    has_s = lat > 0
    halves = 2
    near = lon_count // halves
    far = lat_count * halves
    share = 128 // near
    half = lax.div(lon, jnp.int32(near))
    spot = lon - half * near

    def wrap(at, count):
        return at - count * lax.div(at, jnp.int32(count))

    near_spots = [wrap(spot + d, near) for d in range(near)]
    far_lats = [wrap(lat + d, lat_count) for d in range(lat_count)]
    far_lons = [half * near + spot, (1 - half) * near + spot]

    def along(d):
        return {"lon": half * near + near_spots[d], "lat": lat}

    def across(d):
        return {"lon": far_lons[d % halves], "lat": far_lats[d // halves]}

    north_id = {"lon": lon, "lat": lat + 1}
    south_id = {"lon": lon, "lat": lat - 1}
    east_id = {"lon": east, "lat": lat}
    west_id = {"lon": west, "lat": lat}
    ne_id = {"lon": east, "lat": lat + 1}
    nw_id = {"lon": west, "lat": lat + 1}
    se_id = {"lon": east, "lat": lat - 1}
    sw_id = {"lon": west, "lat": lat - 1}

    barrier = pltpu.get_barrier_semaphore()

    def greet(to):
        pl.semaphore_signal(barrier, inc=1, device_id=to, device_id_type=MESH)

    greet(east_id)
    greet(west_id)

    @pl.when(has_n)
    def _():
        greet(north_id)
        greet(ne_id)
        greet(nw_id)

    @pl.when(has_s)
    def _():
        greet(south_id)
        greet(se_id)
        greet(sw_id)

    for d in range(1, near):
        greet(along(d))
    for d in range(1, far):
        greet(across(d))

    lane24 = lax.broadcasted_iota(jnp.int32, (TALL, COLS), 1)
    row24 = lax.broadcasted_iota(jnp.int32, (TALL, COLS), 0)
    lane = lane24[0:ROWS]
    row = row24[0:ROWS]
    odd_lane = lax.rem(lane, 2) == 1
    low_lane = lane < 64
    place = row24 + jnp.where(row24 < 16, 0, jnp.where(row24 < 20, -19, -5))
    grow = jnp.clip(place + lat * ROWS, 0, lat_count * ROWS - 1).astype(F32)
    phi = LAT_LIMIT * (2.0 * (grow + 0.5) / (lat_count * ROWS) - 1.0)
    sq = phi * phi
    cosine = jnp.ones_like(phi)
    sine = jnp.ones_like(phi)
    for n in range(8, 0, -1):
        cosine = 1.0 - cosine * sq * (1.0 / ((2 * n - 1) * (2 * n)))
        sine = 1.0 - sine * sq * (1.0 / ((2 * n) * (2 * n + 1)))
    inv24 = 1.0 / cosine
    cor24 = sine * phi
    hm24 = 0.5 * inv24
    cc24 = inv24 * inv24
    cor, hm, cc = cor24[0:ROWS], hm24[0:ROWS], cc24[0:ROWS]
    depth = mask[0]
    for l in range(1, LEV):
        depth = depth + mask[l]
    depth_own = depth.astype(F32)
    group = lax.div(lane24, jnp.int32(12))
    slot = lane24 - 12 * group

    def hcopy(e, d):
        if d == 0:
            src, dst, to = row_s.at[e, 0], row_r.at[e, 0], north_id
        elif d == 1:
            src, dst, to = row_s.at[e, 1], row_r.at[e, 1], south_id
        elif d == 2:
            src, dst, to = col_s.at[e], col_r.at[e, 0], east_id
        else:
            src, dst, to = col_s.at[e], col_r.at[e, 1], west_id
        return pltpu.make_async_remote_copy(
            src_ref=src,
            dst_ref=dst,
            send_sem=h_send.at[e, d],
            recv_sem=h_recv.at[e, d],
            device_id=to,
            device_id_type=MESH,
        )

    def launch(e):
        @pl.when(has_n)
        def _():
            hcopy(e, 0).start()

        @pl.when(has_s)
        def _():
            hcopy(e, 1).start()

        hcopy(e, 2).start()
        hcopy(e, 3).start()

    def arrive(e):
        @pl.when(has_s)
        def _():
            hcopy(e, 0).wait_recv()

        @pl.when(has_n)
        def _():
            hcopy(e, 1).wait_recv()

        hcopy(e, 2).wait_recv()
        hcopy(e, 3).wait_recv()

    def drain(e):
        @pl.when(has_n)
        def _():
            hcopy(e, 0).wait_send()

        @pl.when(has_s)
        def _():
            hcopy(e, 1).wait_send()

        hcopy(e, 2).wait_send()
        hcopy(e, 3).wait_send()

    def wcopy(e, d):
        count = 48 if e == 0 else FEAT
        fields = 5 if e == 0 else 4
        if d < 2:
            src = wrow_s.at[e, d, :, 0:count]
            dst = wrow_r.at[e, d, :, 0:count]
            to = (north_id, south_id)[d]
        elif d < 4:
            src = wst_s.at[e, 0:fields]
            dst = wst_r.at[e, d - 2, 0:fields]
            to = (east_id, west_id)[d - 2]
        else:
            src = wc_s.at[e, (d - 4) // 3]
            dst = wc_r.at[e, d - 4]
            to = (north_id, ne_id, nw_id, south_id, se_id, sw_id)[d - 4]
        return pltpu.make_async_remote_copy(
            src_ref=src,
            dst_ref=dst,
            send_sem=w_send.at[e, d],
            recv_sem=w_recv.at[e, d],
            device_id=to,
            device_id_type=MESH,
        )

    north_ones = (0, 4, 5, 6)
    south_ones = (1, 7, 8, 9)

    def wide_launch(e):
        @pl.when(has_n)
        def _():
            for d in north_ones:
                wcopy(e, d).start()

        @pl.when(has_s)
        def _():
            for d in south_ones:
                wcopy(e, d).start()

        wcopy(e, 2).start()
        wcopy(e, 3).start()

    def wide_arrive(e):
        @pl.when(has_s)
        def _():
            for d in north_ones:
                wcopy(e, d).wait_recv()

        @pl.when(has_n)
        def _():
            for d in south_ones:
                wcopy(e, d).wait_recv()

        wcopy(e, 2).wait_recv()
        wcopy(e, 3).wait_recv()

    def wide_drain(e):
        @pl.when(has_n)
        def _():
            for d in north_ones:
                wcopy(e, d).wait_send()

        @pl.when(has_s)
        def _():
            for d in south_ones:
                wcopy(e, d).wait_send()

        wcopy(e, 2).wait_send()
        wcopy(e, 3).wait_send()

    def strip_pack(strip, value, l):
        low = pltpu.roll(value, 12 * l + 3, 1)
        high = pltpu.roll(value, (12 * l + 9) % COLS, 1)
        here = (lane >= 12 * l + 3) & (lane < 12 * l + 6)
        there = (lane >= 12 * l + 6) & (lane < 12 * l + 9)
        return jnp.where(here, low, jnp.where(there, high, strip))

    def wide_stage(e, strips, field_ref, top, count):
        for j in range(3):
            wrow_s[e, 0, j, 0:FEAT] = take_rows(field_ref, top + 13 + j, count)
            wrow_s[e, 1, j, 0:FEAT] = take_rows(field_ref, top + j, count)
            if e == 0:
                wrow_s[e, 0, j, 40:48] = jnp.broadcast_to(depth_own[13 + j : 14 + j], (8, COLS))
                wrow_s[e, 1, j, 40:48] = jnp.broadcast_to(depth_own[j : j + 1], (8, COLS))
        if e > 0:
            wc_s[e] = jnp.zeros((2, 16, COLS), F32)
        for f, strip in enumerate(strips):
            wst_s[e, f] = strip
            wc_s[e, 0, 3 * f : 3 * f + 3] = strip[13:16]
            wc_s[e, 1, 3 * f : 3 * f + 3] = strip[0:3]

    def pick(from_west, own, from_east, slots):
        return jnp.where(
            slots < 3,
            pltpu.roll(from_west, COLS - 6, 1),
            jnp.where(slots >= 9, pltpu.roll(from_east, 6, 1), own),
        )

    def wide_unpack(e):
        k = 3 * e
        if e < 2:
            put_rows(xs.at[k], 7, PAD, wrow_r[e, 0, 2, 0:FEAT])
            put_rows(xs.at[k], 24, PAD, wrow_r[e, 1, 0, 0:FEAT])
            own_ref, top, count, halo_ref = xs.at[k], 8, PAD, xh.at[k]
        else:
            own_ref, top, count, halo_ref = t2, 0, ROWS, t2h
        for j in range(3):
            put_rows(halo_ref, j, 8, wrow_r[e, 0, j, 0:FEAT])
            put_rows(halo_ref, 5 + j, 8, wrow_r[e, 1, j, 0:FEAT])
        put_rows(halo_ref, 3, 8, take_rows(own_ref, top, count))
        put_rows(halo_ref, 4, 8, take_rows(own_ref, top + 15, count))
        slots = slot[0:ROWS]
        below = pick(wc_r[e, 1], wc_r[e, 0], wc_r[e, 2], slots)
        above = pick(wc_r[e, 4], wc_r[e, 3], wc_r[e, 5], slots)
        for f in range(5 if e == 0 else 4):
            own = pick(wst_r[e, 0, f], wst_s[e, f], wst_r[e, 1, f], slots)
            to = t2s.at[f] if e > 1 else (st.at[k, f] if f < 4 else sd)
            to[0:16, :] = own
            to[16:19, :] = below[3 * f : 3 * f + 3]
            to[19:20, :] = own[0:1]
            to[20:21, :] = own[15:16]
            to[21:24, :] = above[3 * f : 3 * f + 3]
        if e == 0:
            dh[3:4] = depth_own[0:1]
            dh[4:5] = depth_own[15:16]
            for j in range(3):
                dh[j : j + 1] = wrow_r[e, 0, j, 40:41]
                dh[5 + j : 6 + j] = wrow_r[e, 1, j, 40:41]

    def take_rows(ref, r, count):
        return ref.reshape(FEAT * count, COLS)[pl.ds(r, FEAT, stride=count), :]

    def put_rows(ref, r, count, value):
        ref.reshape(FEAT * count, COLS)[pl.ds(r, FEAT, stride=count), :] = value

    def pack(packed, value, fl):
        turned = pltpu.roll(value, 2 * fl + 1, 1)
        return jnp.where(lane // 2 == fl, turned, packed)

    def part(at):
        return pl.ds(pl.multiple_of(at * share, share), share)

    def others(stage):
        return range(1, far if stage in (1, 3) else near)

    def fan(stage, d, src, dst, to):
        return pltpu.make_async_remote_copy(
            src_ref=src,
            dst_ref=dst,
            send_sem=a_send.at[stage, d],
            recv_sem=a_recv.at[stage, d],
            device_id=to,
            device_id_type=MESH,
        )

    def fan_copy(stage, d):
        if stage == 0:
            return fan(stage, d, f0, fr1.at[d], along(d))
        if stage == 1:
            return fan(stage, d, f1, fr2.at[d], across(d))
        if stage == 2:
            return fan(stage, d, gb.at[part(near_spots[d])], rs1.at[d], along(d))
        if stage == 3:
            return fan(stage, d, c1, rs2.at[d], across(d))
        return fan(stage, d, c2, ag.at[part(spot)], along(d))

    def fan_start(stage):
        for d in others(stage):
            fan_copy(stage, d).start()

    def fan_arrive(stage):
        for d in others(stage):
            fan_copy(stage, d).wait_recv()

    def fan_drain(stage):
        for d in others(stage):
            fan_copy(stage, d).wait_send()

    def slot_sum(stage, own, slots):
        total = own
        for d in others(stage):
            total = total + slots[d]
        return total

    def levels(body, carry):
        for l in range(LEV):
            carry = body(l, carry)
        return carry

    blank = jnp.zeros((ROWS, COLS), F32)
    strips = [blank] * 5
    for l in range(LEV):
        wet = depth > l
        for f in range(4):
            fl = f * LEV + l
            x = jnp.where(wet, state[fl], 0.0)
            xs[0, fl, 8:24, :] = x
            strips[f] = strip_pack(strips[f], x, l)
        strips[4] = strip_pack(strips[4], depth_own, l)
    wc_s[0] = jnp.zeros((2, 16, COLS), F32)
    wide_stage(0, strips, xs.at[0], 8, PAD)

    def stage_rows(e, north_ref, south_ref):
        row_s[e, 0] = take_rows(north_ref, 23, PAD)
        row_s[e, 1] = take_rows(south_ref, 8, PAD)

    wet_top = depth > 0
    part_flux = jnp.sum(jnp.where(wet_top, flux[...], 0.0), axis=0, keepdims=True)
    part_count = jnp.sum(jnp.where(wet_top, 1.0, 0.0), axis=0, keepdims=True)
    row8 = lax.broadcasted_iota(jnp.int32, (8, COLS), 0)
    f0[...] = jnp.where(
        row8 == 0,
        jnp.broadcast_to(part_flux, (8, COLS)),
        jnp.where(row8 == 1, jnp.broadcast_to(part_count, (8, COLS)), 0.0),
    )

    meet = near + far + 3 * has_n.astype(jnp.int32) + 3 * has_s.astype(jnp.int32)
    pl.semaphore_wait(barrier, meet)
    wide_launch(0)
    fan_start(0)

    @pl.when(jnp.logical_not(has_s))
    def _():
        for e in (0, 3):
            row_r[e, 0] = jnp.zeros((FEAT, COLS), F32)
        for e in range(4):
            wrow_r[e, 0] = jnp.zeros((3, 48, COLS), F32)
            for d in range(3):
                wc_r[e, d] = jnp.zeros((16, COLS), F32)

    @pl.when(jnp.logical_not(has_n))
    def _():
        for e in (0, 3):
            row_r[e, 1] = jnp.zeros((FEAT, COLS), F32)
        for e in range(4):
            wrow_r[e, 1] = jnp.zeros((3, 48, COLS), F32)
            for d in range(3, 6):
                wc_r[e, d] = jnp.zeros((16, COLS), F32)

    def weight(at, value):
        hi, lo = split(value)
        lhs[at, :, 0:64] = hi
        lhs[at, :, 64:128] = hi
        lhs[at, :, 128:192] = lo

    def both(value_ref, rows, cols, plain, turned):
        square[...] = jnp.zeros((COLS, COLS), F32)
        square[0:rows, 0:cols] = value_ref[...]
        whole = square[...]
        weight(plain, whole[0:64, 0:64])
        weight(turned, whole.T[0:64, 0:64])

    def prepare():
        both(wout, FEAT, HID, 2, 3)
        both(wmid, HID, HID, 4, 1)
        both(win, FEAT, HID, 5, 0)
        square[...] = jnp.zeros((COLS, COLS), F32)
        square[0:1, 0:HID] = b_in[...]
        square[1:2, 0:HID] = b_mid[...]
        square[2:3, 0:FEAT] = b_out[...]
        turned = square[...].T
        for at in range(3):
            bcol[at] = jnp.broadcast_to(turned[0:64, at : at + 1], (64, COLS))
        for s in range(2):
            zc[s, FEAT:64, :] = jnp.zeros((64 - FEAT, CELLS), F32)
        dout[FEAT:64, :] = jnp.zeros((64 - FEAT, CELLS), F32)
        gb[112:128] = jnp.zeros((16, COLS), F32)
        put_rows(mn, 7, PAD, jnp.zeros((FEAT, COLS), F32))
        put_rows(pn, 24, PAD, jnp.zeros((FEAT, COLS), F32))

    def product(at, x):
        hi, lo = split(x)
        return jnp.dot(
            lhs[at], jnp.concatenate([hi, lo, hi], axis=0), preferred_element_type=F32
        )

    def bias(at):
        return jnp.concatenate([bcol[at]] * (CHUNK // COLS), axis=1)

    def gather(ref, first, count, out):
        for r in range(ROWS):
            out[0:FEAT, r * COLS : (r + 1) * COLS] = take_rows(ref, first + r, count)

    chunks = [pl.ds(c * CHUNK, CHUNK) for c in range(CELLS // CHUNK)]

    def layer_one(s):
        gather(xs.at[3 * s], 8, PAD, zc.at[s])
        for c in chunks:
            h1[s, :, c] = jnp.tanh(product(0, zc[s, :, c]) + bias(0))

    def layer_two(s):
        for c in chunks:
            h2[s, :, c] = jnp.tanh(product(1, h1[s, :, c]) + bias(1))

    def scatter(ref, n, value):
        for j in range(CHUNK // COLS):
            put_rows(
                ref, n * (CHUNK // COLS) + j, ROWS, value[0:FEAT, j * COLS : (j + 1) * COLS]
            )

    def layer_three(s):
        for n, c in enumerate(chunks):
            scatter(mx, n, product(2, h2[s, :, c]) + bias(2))

    def back_out(s, source):
        def body(l, carry):
            wet = depth > l
            for f in range(4):
                fl = f * LEV + l
                dox[fl] = jnp.where(wet, DT * source[fl], 0.0)
            return carry

        levels(body, 0)
        gather(dox, 0, ROWS, dout)
        for c in chunks:
            h = h2[s, :, c]
            da2[:, c] = product(3, dout[:, c]) * (1.0 - h * h)

    def back_mid(s):
        for c in chunks:
            h = h1[s, :, c]
            da1[:, c] = product(4, da2[:, c]) * (1.0 - h * h)

    def back_in(s):
        for n, c in enumerate(chunks):
            scatter(dx, n, product(5, da1[:, c]))

    def outer(left_ref, right_ref):
        total = jnp.zeros((144, COLS), F32)
        ones = jnp.ones((16, CHUNK), BF16)
        for c in chunks:
            hi, lo = split(left_ref[:, c])
            r_hi, r_lo = split(right_ref[:, c])
            total = total + lax.dot_general(
                jnp.concatenate([hi, lo, ones], axis=0),
                jnp.concatenate([r_hi, r_lo], axis=0),
                (((1,), (1,)), ((), ())),
                preferred_element_type=F32,
            )
        folded = total + pltpu.roll(total, 64, 1)
        return folded[0:64] + total[64:128], folded[128:136]

    def weight_grads(s, add):
        g_in, s_in = outer(zc.at[s], da1)
        g_mid, s_mid = outer(h1.at[s], da2)
        g_out, s_out = outer(h2.at[s], dout)
        wide = lax.broadcasted_iota(jnp.int32, (64, COLS), 1) < 64
        low8 = lax.broadcasted_iota(jnp.int32, (8, COLS), 1) < 64
        top = jnp.where(wide, g_mid, pltpu.roll(g_out, 64, 1))
        low = jnp.where(wide, g_in, 0.0)[0:FEAT]
        sums = jnp.where(
            row8 == 0, s_in, jnp.where(row8 == 1, s_mid, jnp.where(row8 == 2, s_out, 0.0))
        )
        sums = jnp.where(low8, sums, 0.0)
        if add:
            gb[0:64] = gb[0:64] + top
            gb[64:104] = gb[64:104] + low
            gb[104:112] = gb[104:112] + sums
        else:
            gb[0:64] = top
            gb[64:104] = low
            gb[104:112] = sums

    first_lane = lane == 0
    last_lane = lane == COLS - 1

    def add_rows(ref, r, value):
        view = ref.reshape(FEAT * ROWS, COLS)
        view[pl.ds(r, FEAT, stride=ROWS), :] = view[pl.ds(r, FEAT, stride=ROWS), :] + value

    def tendency(f, q, d_x, d_y, sum_x, sum_y, u, v, p_x, p_y, coef):
        c_hm, c_cc, c_cor = coef
        mix = MIX[f]
        change = (
            (mix * c_cc) * (sum_x - 2.0 * q)
            + mix * (sum_y - 2.0 * q)
            - ((u * c_hm) * d_x + (v * 0.5) * d_y)
        )
        if f == 2:
            change = change + (c_cor * v - p_x * c_hm)
        if f == 3:
            change = change - (c_cor * u + p_y * 0.5)
        return DT * change

    def rise(own, edge):
        own_n = jnp.where(
            row == 15, jnp.broadcast_to(edge[5:6], (ROWS, COLS)), pltpu.roll(own, 15, 0)
        )
        own_s = jnp.where(
            row == 0, jnp.broadcast_to(edge[2:3], (ROWS, COLS)), pltpu.roll(own, 1, 0)
        )
        return (
            jnp.concatenate([own_n, pltpu.roll(edge, 7, 0)], axis=0),
            jnp.concatenate([own_s, pltpu.roll(edge, 1, 0)], axis=0),
        )

    def mend(edge, own):
        rows8 = row24[0:8]
        first = jnp.broadcast_to(own[0:1], (8, COLS))
        last = jnp.broadcast_to(own[15:16], (8, COLS))
        return jnp.where(rows8 == 3, first, jnp.where(rows8 == 4, last, edge))

    def strip_section(k):
        start, stage = 3 * (k // 3), k % 3
        wet = (group.astype(F32) < sd[...]) & (lane24 < 12 * LEV)
        q = [st[k, f] for f in range(4)]
        d_x, d_y, sum_x, sum_y = [], [], [], []
        for f in range(4):
            east_q = pltpu.roll(q[f], COLS - 1, 1)
            west_q = pltpu.roll(q[f], 1, 1)
            north_q, south_q = rise(q[f][0:16], q[f][16:24])
            d_x.append(east_q - west_q)
            d_y.append(north_q - south_q)
            sum_x.append(east_q + west_q)
            sum_y.append(north_q + south_q)
            sdx[k, f] = d_x[f]
            sdy[k, f] = d_y[f]

        def down(slope):
            total = GAIN_T * slope[0] + GAIN_S * slope[1]
            for hop in (12, 24, 48, 96):
                total = total + jnp.where(lane24 >= hop, pltpu.roll(total, hop, 1), 0.0)
            return total

        p_x, p_y = down(d_x), down(d_y)
        for f in range(4):
            change = tendency(
                f, q[f], d_x[f], d_y[f], sum_x[f], sum_y[f], q[2], q[3], p_x, p_y,
                (hm24, cc24, cor24),
            )
            moved = q[f] + jnp.where(wet, change, 0.0)
            new = moved if stage == 0 else 0.75 * st[start, f] + 0.25 * moved
            st[k + 1, f, 0:16, :] = new[0:16]
            st[k + 1, f, 16:24, :] = mend(new[16:24], new[0:16])

    def forward(k, forcing):
        e, start, stage = k // 3, 3 * (k // 3), k % 3
        if stage == 0:
            wide_arrive(e)
            wide_unpack(e)
        tall = TALL if stage < 2 else ROWS
        lanes = lane24[0:tall]
        first, last = lanes == 0, lanes == COLS - 1
        coef = (hm24[0:tall], cc24[0:tall], cor24[0:tall])
        if tall == TALL:
            deep = jnp.concatenate([depth_own, dh[...]], axis=0)
        else:
            deep = depth_own
        rows8 = row24[0:8]
        strips = [blank] * 4
        edges = [st[k, f, 0:tall, :] for f in range(4)]
        press_x = press_y = jnp.zeros((tall, COLS), F32)

        def value(at, fl):
            own = xs[at, fl, 8:24, :]
            return jnp.concatenate([own, xh[at, fl]], axis=0) if tall == TALL else own

        for l in range(LEV):
            for f in range(4):
                fl = f * LEV + l
                q = value(k, fl)
                from_w = pltpu.roll(edges[f], (2 * COLS - 2 - 12 * l) % COLS, 1)
                from_e = pltpu.roll(edges[f], (2 * COLS - 10 - 12 * l) % COLS, 1)
                w_side = jnp.where(first, from_w, pltpu.roll(q, 1, 1))
                e_side = jnp.where(last, from_e, pltpu.roll(q, COLS - 1, 1))
                ew[k, fl, 0:tall] = e_side - w_side
                ewsum[fl, 0:tall] = e_side + w_side

        for l in range(LEV):
            wet = deep > float(l)
            u = value(k, 2 * LEV + l)
            v = value(k, 3 * LEV + l)
            for f in range(4):
                fl = f * LEV + l
                q = value(k, fl)
                north = xs[k, fl, 9:25, :]
                south = xs[k, fl, 7:23, :]
                if tall == TALL:
                    edge = xh[k, fl]
                    north = jnp.concatenate([north, pltpu.roll(edge, 7, 0)], axis=0)
                    south = jnp.concatenate([south, pltpu.roll(edge, 1, 0)], axis=0)
                d_x = ew[k, fl, 0:tall]
                d_y = north - south
                ns[k, fl, 0:tall] = d_y
                if f < 2:
                    press_x = press_x + (GAIN_T, GAIN_S)[f] * d_x
                    press_y = press_y + (GAIN_T, GAIN_S)[f] * d_y
                change = tendency(
                    f, q, d_x, d_y, ewsum[fl, 0:tall], north + south, u, v, press_x, press_y, coef
                )
                moved = q + jnp.where(wet, change, 0.0)
                if stage == 0:
                    new = moved
                elif stage == 1:
                    new = 0.75 * value(start, fl) + 0.25 * moved
                else:
                    given = mx[fl]
                    if f == 1 and l == 0:
                        given = given + forcing
                    new = (
                        (1.0 / 3.0) * value(start, fl)
                        + (2.0 / 3.0) * moved
                        + jnp.where(wet, DT * given, 0.0)
                    )
                if stage < 2:
                    own, edge = new[0:ROWS], new[ROWS:TALL]
                    xs[k + 1, fl, 8:24, :] = own
                    xs[k + 1, fl, 7:8, :] = edge[2:3]
                    xs[k + 1, fl, 24:25, :] = edge[5:6]
                    xh[k + 1, fl] = mend(edge, own)
                elif k == 2:
                    xs[k + 1, fl, 8:24, :] = new
                    strips[f] = strip_pack(strips[f], new, l)
                else:
                    fin[fl] = new
        if stage < 2:
            strip_section(k)
        elif k == 2:
            wide_stage(1, strips, xs.at[3], 8, PAD)
            wide_launch(1)

    def give(n, source):
        k, stage = 5 - n, (5 - n) % 3
        scale = (1.0, 0.25, 2.0 / 3.0)[stage]

        def body(t, carry):
            packed, sum_u, sum_v = carry
            l = LEV - 1 - t
            wet = depth > l
            g = [jnp.where(wet, (DT * scale) * source[f * LEV + l], 0.0) for f in range(4)]
            sum_u = sum_u + g[2]
            sum_v = sum_v + g[3]
            u = xs[k, 2 * LEV + l, 8:24, :]
            v = xs[k, 3 * LEV + l, 8:24, :]
            uh = u * hm
            vh = v * 0.5
            push_x = hm * sum_u
            push_y = 0.5 * sum_v
            for f in range(4):
                fl = f * LEV + l
                mix = MIX[f]
                a = uh * g[f]
                b = vh * g[f]
                if f == 0:
                    a = a + GAIN_T * push_x
                    b = b + GAIN_T * push_y
                if f == 1:
                    a = a + GAIN_S * push_x
                    b = b + GAIN_S * push_y
                base = (mix * cc) * g[f]
                plus = base + a
                minus = base - a
                flat = mix * g[f]
                pe[fl] = plus
                mw[fl] = minus
                pn[fl, 8:24, :] = flat + b
                mn[fl, 8:24, :] = flat - b
                packed = pack(packed, jnp.where(low_lane, plus, minus), fl)
            return packed, sum_u, sum_v

        packed, _, _ = levels(body, (blank, blank, blank))
        col_s[n] = packed
        stage_rows(n, mn, pn)
        launch(n)

    def keep(n, source):
        k, stage = 5 - n, (5 - n) % 3
        scale = (1.0, 0.25, 2.0 / 3.0)[stage]
        for l in range(LEV):
            wet = depth > l
            g = [jnp.where(wet, (DT * scale) * source[f * LEV + l], 0.0) for f in range(4)]
            along_x = along_y = blank
            for f in range(4):
                along_x = along_x + g[f] * ew[k, f * LEV + l, 0:ROWS]
                along_y = along_y + g[f] * ns[k, f * LEV + l, 0:ROWS]
            to_u = cor * g[3] + hm * along_x
            to_v = cor * g[2] - 0.5 * along_y
            for f in range(4):
                fl = f * LEV + l
                own = -2.0 * (MIX[f] * cc + MIX[f]) * g[f]
                if f == 2:
                    own = own - to_u
                if f == 3:
                    own = own + to_v
                w_side = jnp.where(first_lane, 0.0, pltpu.roll(mw[fl], 1, 1))
                e_side = jnp.where(last_lane, 0.0, pltpu.roll(pe[fl], COLS - 1, 1))
                acc[fl] = own + w_side + e_side + pn[fl, 9:25, :] + mn[fl, 7:23, :]

    def take(n, source):
        stage = (5 - n) % 3
        e = n
        arrive(e)
        add_rows(acc, 0, row_r[e, 0])
        add_rows(acc, 15, row_r[e, 1])
        received = jnp.where(
            odd_lane, pltpu.roll(col_r[e, 0], 1, 1), pltpu.roll(col_r[e, 1], COLS - 1, 1)
        )

        strips = [blank] * 4
        for l in range(LEV):
            for f in range(4):
                fl = f * LEV + l
                turned = pltpu.roll(received, COLS - 1 - 2 * fl, 1)
                got = acc[fl] + jnp.where(first_lane | last_lane, turned, 0.0)
                new = (2.0 / 3.0) * source[fl] + got
                t2[fl] = new
                strips[f] = strip_pack(strips[f], new, l)
        w = 2 if n == 0 else 3
        wide_stage(w, strips, t2, 0, ROWS)
        wide_launch(w)

    def far_adjoint(k, scale, own_ref, halo_ref, strip_ref, finish, spread):
        deep = jnp.concatenate([depth_own, dh[...]], axis=0)
        wet_s = (group.astype(F32) < sd[...]) & (lane24 < 12 * LEV)
        gs = [jnp.where(wet_s, (DT * scale) * strip_ref[f], 0.0) for f in range(4)]

        def up(total):
            for hop in (12, 24, 48, 96):
                later = pltpu.roll(total, COLS - hop, 1)
                total = total + jnp.where(lane24 < COLS - hop, later, 0.0)
            return total

        def parts(f, g, u, v, sum_u, sum_v):
            a = (u * hm24) * g
            b = (v * 0.5) * g
            if f < 2:
                a = a + (GAIN_T, GAIN_S)[f] * (hm24 * sum_u)
                b = b + (GAIN_T, GAIN_S)[f] * (0.5 * sum_v)
            base = (MIX[f] * cc24) * g
            flat = MIX[f] * g
            return base + a, base - a, flat + b, flat - b

        def local(g, slopes_x, slopes_y):
            along_x = along_y = jnp.zeros((TALL, COLS), F32)
            for f in range(4):
                along_x = along_x + g[f] * slopes_x[f]
                along_y = along_y + g[f] * slopes_y[f]
            given = [-2.0 * (MIX[f] * cc24 + MIX[f]) * g[f] for f in range(4)]
            given[2] = given[2] - (cor24 * g[3] + hm24 * along_x)
            given[3] = given[3] + (cor24 * g[2] - 0.5 * along_y)
            return given

        up_u, up_v = up(gs[2]), up(gs[3])
        side = [parts(f, gs[f], st[k, 2], st[k, 3], up_u, up_v) for f in range(4)]
        if spread:
            given = local(gs, [sdx[k, f] for f in range(4)], [sdy[k, f] for f in range(4)])
            for f in range(4):
                plus, minus, to_s, to_n = side[f]
                north_s, _ = rise(to_s[0:16], to_s[16:24])
                _, south_s = rise(to_n[0:16], to_n[16:24])
                new = scale * strip_ref[f] + given[f] + north_s + south_s
                new = new + pltpu.roll(plus, COLS - 1, 1) + pltpu.roll(minus, 1, 1)
                t1s[f, 0:16, :] = new[0:16]
                t1s[f, 16:24, :] = mend(new[16:24], new[0:16])
        for f in range(4):
            tp[f] = side[f][0]
            tm[f] = side[f][1]

        sum_u = sum_v = jnp.zeros((TALL, COLS), F32)
        for l in range(LEV - 1, -1, -1):
            wet = deep > float(l)
            at = [f * LEV + l for f in range(4)]
            g = []
            for fl in at:
                x = jnp.concatenate([own_ref[fl], halo_ref[fl]], axis=0)
                g.append(jnp.where(wet, (DT * scale) * x, 0.0))
            sum_u = sum_u + g[2]
            sum_v = sum_v + g[3]
            u = jnp.concatenate([xs[k, at[2], 8:24, :], xh[k, at[2]]], axis=0)
            v = jnp.concatenate([xs[k, at[3], 8:24, :], xh[k, at[3]]], axis=0)
            given = local(g, [ew[k, fl] for fl in at], [ns[k, fl] for fl in at])
            for f, fl in enumerate(at):
                plus, minus, to_s, to_n = parts(f, g[f], u, v, sum_u, sum_v)
                pe24[fl] = plus
                mw24[fl] = minus
                acc24[fl] = given[f]
                pn[fl, 8:24, :] = to_s[0:16]
                mn[fl, 8:24, :] = to_n[0:16]
                pn[fl, 24:25, :] = to_s[21:22]
                mn[fl, 7:8, :] = to_n[18:19]
                pnh[fl] = to_s[16:24]
                mnh[fl] = to_n[16:24]
        first24, last24 = lane24 == 0, lane24 == COLS - 1
        for l in range(LEV):
            for f in range(4):
                fl = f * LEV + l
                from_w = pltpu.roll(tm[f], (2 * COLS - 2 - 12 * l) % COLS, 1)
                from_e = pltpu.roll(tp[f], (2 * COLS - 10 - 12 * l) % COLS, 1)
                w_side = jnp.where(first24, from_w, pltpu.roll(mw24[fl], 1, 1))
                e_side = jnp.where(last24, from_e, pltpu.roll(pe24[fl], COLS - 1, 1))
                got = acc24[fl] + w_side + e_side
                own = got[0:16] + pn[fl, 9:25, :] + mn[fl, 7:23, :]
                edge = None
                if spread:
                    edge = got[16:24] + pltpu.roll(pnh[fl], 7, 0) + pltpu.roll(mnh[fl], 1, 0)
                finish(fl, l, own, edge)

    def back_two(e, source):
        k = 3 * (3 - e)

        def middle(fl, l, own, edge):
            new = 0.25 * t2[fl] + own
            t1[fl] = new
            t1h[fl] = mend(0.25 * t2h[fl] + edge, new)

        def start(fl, l, own, edge):
            new = (1.0 / 3.0) * source[fl] + 0.75 * t2[fl] + t1[fl] + own + dx[fl]
            if k == 0:
                grad[fl] = jnp.where(depth > l, new, 0.0)
            else:
                lam[fl] = new

        wide_unpack(e)
        far_adjoint(k + 1, 0.25, t2, t2h, t2s, middle, True)
        far_adjoint(k, 1.0, t1, t1h, t1s, start, False)
        if k > 0:
            put_rows(mn, 7, PAD, jnp.zeros((FEAT, COLS), F32))
            put_rows(pn, 24, PAD, jnp.zeros((FEAT, COLS), F32))

    prepare()
    layer_one(0)
    layer_two(0)
    layer_three(0)
    fan_arrive(0)
    f1[...] = slot_sum(0, f0[...], fr1)
    fan_start(1)
    forward(0, None)
    forward(1, None)
    fan_arrive(1)
    totals = slot_sum(1, f1[...], fr2)
    flux_sum = jnp.sum(totals[0:1, :], axis=1, keepdims=True)
    count_sum = jnp.sum(totals[1:2, :], axis=1, keepdims=True)
    mean = jnp.broadcast_to(flux_sum / count_sum, (ROWS, COLS))
    forcing = -FRESHWATER * (flux[...] - mean)
    forward(2, forcing)
    layer_one(1)
    layer_two(1)
    layer_three(1)
    back_out(1, cot)
    back_mid(1)
    back_in(1)
    forward(3, None)
    forward(4, None)

    give(0, cot)
    forward(5, forcing)
    keep(0, cot)
    take(0, cot)
    weight_grads(1, False)
    wide_arrive(2)
    back_two(2, cot)
    give(3, lam)
    keep(3, lam)
    back_out(0, lam)
    back_mid(0)
    weight_grads(0, True)
    fan_start(2)
    back_in(0)
    take(3, lam)
    fan_arrive(2)
    c1[...] = slot_sum(2, gb[part(spot)], rs1)
    fan_start(3)
    wide_arrive(3)
    fan_arrive(3)
    scale = 1.0 / math.sqrt(lat_count * ROWS * lon_count * COLS)
    c2[...] = slot_sum(3, c1[...], rs2) * scale
    ag[part(spot)] = c2[...]
    fan_start(4)
    back_two(3, lam)
    for e in (0, 3):
        drain(e)
    for e in range(4):
        wide_drain(e)
    for stage in range(4):
        fan_drain(stage)
    fan_arrive(4)
    fan_drain(4)


def unpack(fin, grad, ag, o_fin, o_grad, g_win, g_bin, g_wmid, g_bmid, g_wout, g_bout):
    o_fin[...] = fin[...]
    o_grad[...] = grad[...]
    g_wmid[...] = ag[0:64, 0:HID]
    g_wout[...] = pltpu.roll(ag[0:COLS], 64, 1).T[0:FEAT, 0:HID]
    g_win[...] = ag[64:104, 0:HID]
    sums = ag[104:112]
    g_bin[...] = sums[0:1, 0:HID]
    g_bmid[...] = sums[1:2, 0:HID]
    g_bout[...] = sums[2:3, 0:FEAT]


def on_device(lat_count, lon_count, state, mask, flux, win, b_in, wmid, b_mid, wout, b_out, cot):
    def v(*shape):
        return pltpu.VMEM(shape, F32)

    near, far = lon_count // 2, lat_count * 2
    share = 128 // near
    vmem = pl.BlockSpec(memory_space=pltpu.VMEM)
    field = (FEAT, ROWS, COLS)
    tall = (FEAT, PAD, COLS)
    wide = (64, CELLS)
    out = pl.pallas_call(
        functools.partial(kernel, lat_count, lon_count),
        out_shape=[jax.ShapeDtypeStruct(shape, F32) for shape in (field, field, (128, COLS))],
        in_specs=[vmem] * 10,
        out_specs=[vmem] * 3,
        scratch_shapes=[
            v(6, *tall),
            v(FEAT, TALL, COLS),
            v(6, FEAT, TALL, COLS),
            v(6, FEAT, TALL, COLS),
            v(*field),
            v(*field),
            v(*tall),
            v(*tall),
            v(*field),
            v(*field),
            v(*field),
            v(*field),
            v(2, *wide),
            v(2, *wide),
            v(2, *wide),
            v(*wide),
            v(*wide),
            v(*wide),
            v(*field),
            v(*field),
            v(*field),
            pltpu.VMEM((6, 64, 192), BF16),
            v(3, 64, COLS),
            v(COLS, COLS),
            v(128, COLS),
            v(near, share, COLS),
            v(share, COLS),
            v(far, share, COLS),
            v(share, COLS),
            v(8, COLS),
            v(near, 8, COLS),
            v(8, COLS),
            v(far, 8, COLS),
            v(6, 2, FEAT, COLS),
            v(6, 2, FEAT, COLS),
            v(6, ROWS, COLS),
            v(6, 2, ROWS, COLS),
            v(6, FEAT, 8, COLS),
            v(6, 4, TALL, COLS),
            v(TALL, COLS),
            v(8, COLS),
            v(4, 2, 3, 48, COLS),
            v(4, 2, 3, 48, COLS),
            v(4, 5, ROWS, COLS),
            v(4, 2, 5, ROWS, COLS),
            v(4, 2, 16, COLS),
            v(4, 6, 16, COLS),
            v(FEAT, 8, COLS),
            v(FEAT, 8, COLS),
            v(4, TALL, COLS),
            v(4, TALL, COLS),
            v(4, TALL, COLS),
            v(4, TALL, COLS),
            v(6, 4, TALL, COLS),
            v(6, 4, TALL, COLS),
            v(FEAT, TALL, COLS),
            v(FEAT, TALL, COLS),
            v(FEAT, TALL, COLS),
            v(FEAT, 8, COLS),
            v(FEAT, 8, COLS),
            pltpu.SemaphoreType.DMA((6, 4)),
            pltpu.SemaphoreType.DMA((6, 4)),
            pltpu.SemaphoreType.DMA((4, 10)),
            pltpu.SemaphoreType.DMA((4, 10)),
            pltpu.SemaphoreType.DMA((5, max(near, far))),
            pltpu.SemaphoreType.DMA((5, max(near, far))),
        ],
        compiler_params=pltpu.CompilerParams(
            collective_id=0, has_side_effects=True, vmem_limit_bytes=60 * 1024 * 1024
        ),
    )(
        state.reshape(field),
        mask,
        flux,
        win,
        b_in.reshape(1, HID),
        wmid,
        b_mid.reshape(1, HID),
        wout.T,
        b_out.reshape(1, FEAT),
        cot.reshape(field),
    )
    out = pl.pallas_call(
        unpack,
        out_shape=[
            jax.ShapeDtypeStruct(shape, F32)
            for shape in (
                field,
                field,
                (FEAT, HID),
                (1, HID),
                (HID, HID),
                (1, HID),
                (FEAT, HID),
                (1, FEAT),
            )
        ],
        in_specs=[vmem] * 3,
        out_specs=[vmem] * 8,
    )(*out)
    shape4 = (4, LEV, ROWS, COLS)
    return (
        out[0].reshape(shape4),
        out[1].reshape(shape4),
        out[2],
        out[3].reshape(HID),
        out[4],
        out[5].reshape(HID),
        out[6].T,
        out[7].reshape(FEAT),
    )


def solution(mesh):
    block = P(None, None, "lat", "lon")
    return jax.shard_map(
        functools.partial(on_device, mesh.shape["lat"], mesh.shape["lon"]),
        mesh=mesh,
        in_specs=(
            block,
            P(None, "lat", "lon"),
            P("lat", "lon"),
            P(),
            P(),
            P(),
            P(),
            P(),
            P(),
            block,
        ),
        out_specs=(block, block, P(), P(), P(), P(), P(), P()),
        check_vma=False,
    )
```
